32 devices in a mesh: frames: 8 (over y, x, core), coils: 4 (over z).
Axes of the slice: x: 2, y: 2, z: 4, core: 2. Of those that a mesh axis runs over, the one named last changes fastest.
Arguments:
- kdata: bfloat16 [32, 32, 2, 13, 256], P('frames', 'coils'), may hold values from -6 to 6
- angles: int32 [32, 13], P('frames'), may hold values from 0 to 15
- kernels: bfloat16 [2, 16, 256, 128], replicated, may hold values from 0 to 1.5, as said below
- seg_bounds: int32 [2], replicated, may hold values from 64 to 191, as said below
- sensitivity: bfloat16 [32, 2, 128, 128], P('coils'), may hold values from -1 to 1
- ref_center: float32 [32, 2], P('coils'), may hold values from -24 to 24
- projection: float32 [3, 32], P(None, 'coils'), may hold values from -1 to 1
- init_coef: float32 [3], replicated, may hold values from -6 to 6
Outputs:
- image: float32 [32, 2, 128, 128], P('frames', None, 'coils')
- field_coef: float32 [32, 3], P('frames')
The draws below stay inside these ranges and needn't reach their ends.
Inputs may be any that keep to these rules, and one draw needn't show every extreme that they name: `kernels`: entries are not negative. `seg_bounds`: strictly increasing; bound j lies within 21 of j * 85, counting j from 1.
All inputs are finite; a program needn't handle non-finite values.
Results may differ from the reference program's by a relative error of at most 0.0059.
Values sent between devices are 32-bit elements; how exact they have to be, the bound alone decides.
No kernel may reach another device: no remote copies, remote signals or barrier semaphores. Data moves between devices by JAX's collectives and lax.ppermute only.
A program may use at most 64 MiB of HBM per device.

```python
import math
import jax
import jax.numpy as jnp
from jax import lax

G = 128
R = 256
COILS = 32
SPOKES = 13
NA = 16
SEGS = 3
BASIS = 3
FRAMES = 32


def draw_kernels(key, part):
    subkeys = jax.random.split(key, 2)
    angles_rad = math.pi * jnp.arange(NA, dtype=jnp.float32) / NA
    radial_pos = (jnp.arange(R, dtype=jnp.float32) - R // 2) * (G / R) * 0.95
    cells = jnp.arange(G, dtype=jnp.float32)

    def spread_kernel(direction, subkey):
        center_pos = G // 2 + radial_pos[None, :] * direction[:, None]
        offset = cells[None, None, :] - center_pos[:, :, None]
        profile = jnp.exp(-0.5 * (offset / 1.2) ** 2) * (jnp.abs(offset) <= 3.0)
        jitter = jax.random.uniform(subkey, profile.shape, jnp.float32, 0.5, 1.5)
        return profile * jitter
    stacked = jnp.stack([spread_kernel(jnp.cos(angles_rad), subkeys[0]), spread_kernel(jnp.sin(angles_rad), subkeys[1])])
    return stacked.astype(jnp.bfloat16)


def draw_seg_bounds(key, part):
    spacing = R // SEGS
    jitter = R // (4 * SEGS)
    nominal = jnp.arange(1, SEGS, dtype=jnp.int32) * spacing
    return nominal + jax.random.randint(key, (SEGS - 1,), -jitter, jitter + 1, dtype=jnp.int32)


def touch_ends(array, rng, least, top_value):
    longest = array.shape.index(max(array.shape))
    spots = []
    for shift in (0, 1):
        where = [jax.random.randint(jax.random.fold_in(rng, axis), (), 0, length) for axis, length in enumerate(array.shape)]
        where[longest] = (where[longest] + shift) % array.shape[longest]
        spots.append(tuple(where))
    return array.at[spots[0]].set(least).at[spots[1]].set(top_value)


def levels(stream_key, shape, cuts, least, high):
    factor_of = 1.0
    for axis_at, shards_of in cuts:
        heights = jax.random.uniform(jax.random.fold_in(jax.random.fold_in(stream_key, 6), axis_at), (shards_of,), jnp.float32, least / len(cuts), high / len(cuts))
        factor_of = factor_of * jnp.repeat(jnp.exp(heights), shape[axis_at] // shards_of).reshape((-1,) + (1,) * (len(shape) - 1 - axis_at))
    return factor_of


def noise(key, shape, spread, bound, shards=(), held_as=jnp.bfloat16):
    level = levels(key, shape, shards, -0.22, 0.18) if shards else 1.0
    entries = jax.random.normal(key, shape, jnp.float32) * spread * level
    return jnp.minimum(jnp.maximum(entries, -bound), bound).astype(held_as)


def setup_inputs(seed: int = 0) -> dict:
    seeds = jax.random.split(jax.random.key(seed), 9)
    kdata = noise(seeds[0], (FRAMES, COILS, 2, SPOKES, R), 1.0, 6.0, ((0, 8), (1, 4)))
    angles = touch_ends(jax.random.randint(seeds[1], (FRAMES, SPOKES), 0, NA), jax.random.fold_in(seeds[1], 1), 0, NA - 1).astype(jnp.int32)
    kernels = draw_kernels(jax.random.fold_in(seeds[8], 71), 0)
    seg_bounds = draw_seg_bounds(jax.random.fold_in(seeds[8], 71), 0)
    sensitivity = noise(seeds[4], (COILS, 2, G, G), COILS ** -0.5, 1.0, ((0, 4),))
    ref_center = noise(seeds[5], (COILS, 2), 4.0, 24.0, ((0, 4),), jnp.float32)
    projection = noise(seeds[6], (BASIS, COILS), COILS ** -0.5, 1.0, ((1, 4),), jnp.float32)
    init_coef = jnp.clip(jax.random.uniform(seeds[7], (BASIS,), jnp.float32, -6.0, 6.0), -6.0, 6.0)
    return {"kdata": kdata, "angles": angles, "kernels": kernels, "seg_bounds": seg_bounds, "sensitivity": sensitivity, "ref_center": ref_center, "projection": projection, "init_coef": init_coef}


def dft_tables(grid_side):
    offsets = jnp.arange(grid_side, dtype=jnp.int32) - grid_side // 2
    wrapped = jnp.mod(offsets[:, None] * offsets[None, :], grid_side).astype(jnp.float32)
    phase_arg = (2.0 * math.pi / grid_side) * wrapped
    cosine = (jnp.cos(phase_arg) / grid_side).astype(jnp.bfloat16)
    sine = (jnp.sin(phase_arg) / grid_side).astype(jnp.bfloat16)
    right_table = jnp.stack([jnp.stack([cosine, sine]), jnp.stack([-sine, cosine])])
    left_table = jnp.stack([jnp.stack([cosine, -sine]), jnp.stack([sine, cosine])])
    return right_table, left_table


def segment_times(seg_bounds, readout):
    seg_edges = jnp.concatenate([jnp.zeros((1,), jnp.int32), seg_bounds.astype(jnp.int32), jnp.full((1,), readout, jnp.int32)])
    centers = (seg_edges[:-1] + seg_edges[1:] - 1).astype(jnp.float32) / (2.0 * readout)
    return seg_edges, centers


def modulate(partials, field_coef, seg_times, row_start, grid_side):
    row_count = partials.shape[-2]
    half_side = grid_side // 2
    row_pos = (row_start + jnp.arange(row_count, dtype=jnp.int32) - half_side).astype(jnp.float32) / half_side
    col_pos = (jnp.arange(grid_side, dtype=jnp.int32) - half_side).astype(jnp.float32) / half_side
    field_map = field_coef[:, 0, None, None] + field_coef[:, 1, None, None] * row_pos[None, :, None] + field_coef[:, 2, None, None] * col_pos[None, None, :]
    turned = field_map[:, None] * seg_times[None, :, None, None]
    cos_turn = jnp.cos(turned)
    sin_turn = jnp.sin(turned)
    real_part = jnp.sum(cos_turn * partials[:, :, 0] - sin_turn * partials[:, :, 1], axis=1)
    imag_part = jnp.sum(sin_turn * partials[:, :, 0] + cos_turn * partials[:, :, 1], axis=1)
    return jnp.stack([real_part, imag_part], axis=1)


def frame_images(frame_data, frame_angles, kernels, sensitivity, seg_edges, right_table, left_table):
    readout = frame_data.shape[3]
    weights_x = kernels[0][frame_angles].astype(jnp.float32)
    weights_y = kernels[1][frame_angles].astype(jnp.float32)
    weighted = (frame_data.astype(jnp.float32)[:, :, :, :, None] * weights_y[None, None]).astype(jnp.bfloat16).astype(jnp.float32)
    readout_index = jnp.arange(readout, dtype=jnp.int32)
    sens_real = sensitivity[:, 0].astype(jnp.float32)
    sens_imag = sensitivity[:, 1].astype(jnp.float32)
    right_wide = right_table.astype(jnp.float32)
    left_wide = left_table.astype(jnp.float32)
    results = []
    for segment in range(seg_edges.shape[0] - 1):
        inside = (readout_index >= seg_edges[segment]) & (readout_index < seg_edges[segment + 1])
        masked_x = jnp.where(inside[None, :, None], weights_x, jnp.zeros((), jnp.float32))
        gridded = jnp.einsum("srx,cpsry->xcpy", masked_x, weighted).astype(jnp.bfloat16).astype(jnp.float32)
        half_image = jnp.einsum("xcpg,pqgy->xcqy", gridded, right_wide).astype(jnp.bfloat16).astype(jnp.float32)
        coil_image = jnp.einsum("qpzx,xcpy->cqzy", left_wide, half_image)
        combined_real = jnp.sum(sens_real * coil_image[:, 0] + sens_imag * coil_image[:, 1], axis=0)
        combined_imag = jnp.sum(sens_real * coil_image[:, 1] - sens_imag * coil_image[:, 0], axis=0)
        results.append(jnp.stack([combined_real, combined_imag]))
    return jnp.stack(results)


def reference(kdata, angles, kernels, seg_bounds, sensitivity, ref_center, projection, init_coef):
    readout = kdata.shape[4]
    grid_side = kernels.shape[3]
    center = jnp.sum(kdata[..., readout // 2].astype(jnp.float32), axis=3)
    previous = jnp.concatenate([ref_center[None], center[:-1]], axis=0)
    cross_term = previous[..., 0] * center[..., 1] - previous[..., 1] * center[..., 0]
    energy = jnp.sum(previous * previous, -1) + jnp.sum(center * center, -1) + 1.0
    drift_signal = 2.0 * cross_term / energy
    increment = jnp.dot(drift_signal, projection.T, precision=lax.Precision.HIGHEST)
    field_coef = init_coef[None, :] + jnp.cumsum(increment, axis=0)
    seg_edges, seg_times = segment_times(seg_bounds, readout)
    right_table, left_table = dft_tables(grid_side)

    def per_frame(inputs):
        frame_data, frame_angles, frame_coef = inputs
        partial_img = frame_images(frame_data, frame_angles, kernels, sensitivity, seg_edges, right_table, left_table)
        return modulate(partial_img[None], frame_coef[None], seg_times, 0, grid_side)[0]

    image = lax.map(per_frame, (kdata, angles, field_coef))
    return image, field_coef
```

```python
import functools
import math

import jax
import jax.numpy as jnp
import ml_dtypes
import numpy as np
from jax import lax
from jax.experimental import pallas as pl
from jax.experimental.pallas import tpu as pltpu
from jax.sharding import PartitionSpec as P

BF16 = jnp.bfloat16
F32 = jnp.float32


def dft_tables(side):
    offsets = np.arange(side) - side // 2
    wrapped = np.mod(offsets[:, None] * offsets[None, :], side).astype(np.float32)
    phase = np.float32(2.0 * math.pi / side) * wrapped
    cosine = (np.cos(phase) / np.float32(side)).astype(ml_dtypes.bfloat16)
    sine = (np.sin(phase) / np.float32(side)).astype(ml_dtypes.bfloat16)
    right = np.block([[cosine, sine], [-sine, cosine]])
    left = np.block([[cosine, -sine], [sine, cosine]])
    return right, left


def windows(readout, segs):
    spacing, jitter = readout // segs, readout // (4 * segs)
    low = [0] + [j * spacing - jitter for j in range(1, segs)]
    high = [j * spacing + jitter for j in range(1, segs)] + [readout]
    width = 128
    while True:
        starts = [max(0, min(a // 16 * 16, readout - width)) for a in low]
        if all(s + width >= b for s, b in zip(starts, high)) or width >= readout:
            return starts, min(width, readout)
        width += 128


def edges_of(bounds_ref, readout, segs):
    return [0] + [bounds_ref[j] for j in range(segs - 1)] + [readout]


def prepare(starts, width, bounds_ref, kdata_ref, kx_ref, rows_ref, center_ref):
    angles, readout, side = kx_ref.shape
    segs = len(starts)
    edges = edges_of(bounds_ref, readout, segs)
    index = lax.broadcasted_iota(jnp.int32, (side, width), 1)
    keep = []
    for l in range(segs):
        at = index + starts[l]
        keep.append((at >= edges[l]) & (at < edges[l + 1]))

    def one(a, carry):
        for l in range(segs):
            part = kx_ref[a, starts[l] : starts[l] + width, :].astype(F32)
            rows_ref[a, l] = jnp.where(keep[l], part.T, 0.0).astype(BF16)
        return carry

    lax.fori_loop(0, angles, one, 0)
    half = readout // 2
    lanes = center_ref.shape[-1]
    for t in range(kdata_ref.shape[0]):
        for c in range(kdata_ref.shape[1]):
            total = jnp.zeros((2, lanes), F32)
            for s in range(kdata_ref.shape[2]):
                total += kdata_ref[t, c, s, :, half : half + lanes].astype(F32)
            center_ref[t, 0, c, :] = total[0]
            center_ref[t, 1, c, :] = total[1]


def drift(position_ref, center_ref, arrived_ref, first_ref, projection_ref, step_ref):
    frames, _, coils, lanes = center_ref.shape
    basis = projection_ref.shape[0]
    at_start = position_ref[0] == 0
    for t in range(frames):
        if t == 0:
            before = [jnp.where(at_start, first_ref[p], arrived_ref[p]) for p in range(2)]
        else:
            before = [center_ref[t - 1, p] for p in range(2)]
        now = [center_ref[t, p] for p in range(2)]
        cross = before[0] * now[1] - before[1] * now[0]
        energy = before[0] * before[0] + before[1] * before[1]
        energy = energy + (now[0] * now[0] + now[1] * now[1]) + 1.0
        signal = 2.0 * cross / energy
        for b in range(basis):
            row = jnp.sum(projection_ref[b] * signal, axis=0, keepdims=True)
            step_ref[pl.ds(t * basis + b, 1), :] = row


def grid_frames(
    starts, width, angles_ref, kdata_ref, rows_ref, ky_ref, right_ref, left_ref, sens_ref,
    out_ref, kd_ref, lhs_ref, turned_ref, weighted_ref, half_ref, *, first
):
    coils, spokes, _, readout = kdata_ref.shape
    segs = len(starts)
    side = ky_ref.shape[2]
    t = pl.program_id(0) + first
    slots = kd_ref.shape[1] // 2
    for s in range(spokes):
        a = angles_ref[t, s]
        for l in range(segs):
            lhs_ref[l, :, s * width : (s + 1) * width] = rows_ref[a, l]
        for c in range(coils):
            kd_ref[c, 2 * s : 2 * s + 2, :] = kdata_ref[c, s].astype(F32)
    per = min(128 // (2 * slots), coils)
    for g in range(coils // per):
        block = kd_ref[g * per : (g + 1) * per].reshape(per * 2 * slots, readout)
        flipped = block.T
        for j in range(per):
            turned_ref[g * per + j, :, : 2 * slots] = flipped[:, j * 2 * slots : (j + 1) * 2 * slots].astype(BF16)
    out_ref[...] = jnp.zeros_like(out_ref)

    def coil(c, carry):
        columns = turned_ref[c]
        for s in range(spokes):
            ky = ky_ref[angles_ref[t, s]]
            for p in range(2):
                scale = jnp.broadcast_to(columns[:, 2 * s + p : 2 * s + p + 1], (readout, side))
                weighted_ref[s, :, p * side : (p + 1) * side] = scale * ky
        for l in range(segs):
            rhs = weighted_ref[:, starts[l] : starts[l] + width, :].reshape(spokes * width, 2 * side)
            gridded = jnp.dot(lhs_ref[l], rhs, preferred_element_type=F32).astype(BF16)
            half = jnp.dot(gridded, right_ref[...], preferred_element_type=F32).astype(BF16)
            half_ref[:side, l * side : (l + 1) * side] = half[:, :side]
            half_ref[side:, l * side : (l + 1) * side] = half[:, side:]
        image = jnp.dot(left_ref[...], half_ref[...], preferred_element_type=F32)
        real = sens_ref[c, 0].astype(F32)
        imag = sens_ref[c, 1].astype(F32)
        for l in range(segs):
            re = image[:side, l * side : (l + 1) * side]
            im = image[side:, l * side : (l + 1) * side]
            out_ref[l, 0] += real * re + imag * im
            out_ref[l, 1] += real * im - imag * re
        return carry

    lax.fori_loop(0, coils, coil, 0)


def modulate(side, readout, position_ref, bounds_ref, coef_ref, parts_ref, *out_refs):
    segs = parts_ref.shape[1]
    owners = len(out_refs)
    rows = side // owners
    half = side // 2
    me = position_ref[0]
    edges = edges_of(bounds_ref, readout, segs)
    times = [(edges[l] + edges[l + 1] - 1).astype(F32) / (2.0 * readout) for l in range(segs)]
    t = pl.program_id(0)
    f0, f1, f2 = coef_ref[t, 0], coef_ref[t, 1], coef_ref[t, 2]
    col = (lax.broadcasted_iota(jnp.int32, (8, side), 1) - half).astype(F32) / half
    pos = (lax.broadcasted_iota(jnp.int32, (side, 128), 0) - half).astype(F32) / half
    factors = []
    for l in range(segs):
        down = (f0 + f1 * pos) * times[l]
        across = (f2 * col) * times[l]
        factors.append((jnp.cos(down)[:, :1], jnp.sin(down)[:, :1], jnp.cos(across)[:1], jnp.sin(across)[:1]))
    image_re = jnp.zeros((side, side), F32)
    image_im = jnp.zeros((side, side), F32)
    for l in range(segs):
        cr, sr, cc, sc = factors[l]
        cos = cr * cc - sr * sc
        sin = sr * cc + cr * sc
        re, im = parts_ref[0, l, 0], parts_ref[0, l, 1]
        image_re += cos * re - sin * im
        image_im += sin * re + cos * im
    for owner in range(owners):
        for d, out_ref in enumerate(out_refs):

            @pl.when(lax.rem(me + d, owners) == owner)
            def _():
                out_ref[0, 0] = image_re[owner * rows : (owner + 1) * rows]
                out_ref[0, 1] = image_im[owner * rows : (owner + 1) * rows]


def shifted(block, axis, distance):
    count = lax.axis_size(axis)
    return lax.ppermute(block, axis, [(i, i + distance) for i in range(count - distance)])


def around(block, axis, distance):
    count = lax.axis_size(axis)
    return lax.ppermute(block, axis, [(i, (i + distance) % count) for i in range(count)])


def local(kdata, angles, kernels, seg_bounds, sensitivity, ref_center, projection, init_coef):
    frames, coils, _, spokes, readout = kdata.shape
    table, side = kernels.shape[1], kernels.shape[3]
    segs = seg_bounds.shape[0] + 1
    basis = projection.shape[0]
    owners = lax.axis_size("coils")
    starts, width = windows(readout, segs)
    right, left = (jnp.asarray(table) for table in dft_tables(side))
    kd = jnp.swapaxes(kdata, 2, 3)
    smem = pl.BlockSpec(memory_space=pltpu.SMEM)
    vmem = pl.BlockSpec(memory_space=pltpu.VMEM)
    place = lax.axis_index("frames").astype(jnp.int32).reshape(1)
    owner = lax.axis_index("coils").astype(jnp.int32).reshape(1)

    rows, center = pl.pallas_call(
        functools.partial(prepare, starts, width),
        out_shape=(
            jax.ShapeDtypeStruct((table, segs, side, width), BF16),
            jax.ShapeDtypeStruct((frames, 2, coils, 128), F32),
        ),
        in_specs=[smem, vmem, vmem],
        out_specs=(vmem, vmem),
        name="prepare",
    )(seg_bounds, kd, kernels[0])

    arrived = shifted(center[-1], "frames", 1)
    first = jnp.broadcast_to(ref_center.T[:, :, None], (2, coils, 128))
    weights = jnp.broadcast_to(projection[:, :, None], (basis, coils, 128))
    step = pl.pallas_call(
        drift,
        out_shape=jax.ShapeDtypeStruct((frames * basis, 128), F32),
        in_specs=[smem, vmem, vmem, vmem, vmem],
        out_specs=vmem,
        name="drift",
    )(place, center, arrived, first, weights)
    step = step[:, :1].reshape(frames, basis)
    distance = 1
    increment = step
    while distance < owners:
        pairs = [(i, i ^ distance) for i in range(owners)]
        increment = increment + lax.ppermute(increment, "coils", pairs)
        distance *= 2
    running = jnp.sum(increment, axis=0)
    before = jnp.zeros_like(running)
    distance = 1
    while distance < lax.axis_size("frames"):
        came = shifted(running, "frames", distance)
        running, before = running + came, before + came
        distance *= 2
    field_coef = init_coef[None, :] + (before[None, :] + jnp.cumsum(increment, axis=0))

    def gridded(begin, end):
        count = end - begin
        grid_spec = pltpu.PrefetchScalarGridSpec(
            num_scalar_prefetch=1,
            grid=(count,),
            in_specs=[
                pl.BlockSpec((None, coils, spokes, 2, readout), lambda i, _: (begin + i, 0, 0, 0, 0)),
                vmem,
                pl.BlockSpec((None, table, readout, side), lambda i, _: (1, 0, 0, 0)),
                vmem,
                vmem,
                vmem,
            ],
            out_specs=pl.BlockSpec((None, segs, 2, side, side), lambda i, _: (i, 0, 0, 0, 0)),
            scratch_shapes=[
                pltpu.VMEM((coils, 32, readout), F32),
                pltpu.VMEM((segs, side, spokes * width), BF16),
                pltpu.VMEM((coils, readout, 128), BF16),
                pltpu.VMEM((spokes, readout, 2 * side), BF16),
                pltpu.VMEM((2 * side, segs * side), BF16),
            ],
        )
        return pl.pallas_call(
            functools.partial(grid_frames, starts, width, first=begin),
            out_shape=jax.ShapeDtypeStruct((count, segs, 2, side, side), F32),
            grid_spec=grid_spec,
            name="gridding",
        )(angles, kd, rows, kernels, right, left, sensitivity)

    def images(parts, coef):
        count = parts.shape[0]
        block = jax.ShapeDtypeStruct((count, 2, side // owners, side), F32)
        spec = pl.BlockSpec((1, 2, side // owners, side), lambda i: (i, 0, 0, 0))
        blocks = pl.pallas_call(
            functools.partial(modulate, side, readout),
            out_shape=(block,) * owners,
            grid=(count,),
            in_specs=[smem, smem, smem, pl.BlockSpec((1, segs, 2, side, side), lambda i: (i, 0, 0, 0, 0))],
            out_specs=(spec,) * owners,
            name="modulate",
        )(owner, seg_bounds, coef, parts)
        total = blocks[0]
        for d in range(1, owners):
            total = total + around(blocks[d], "coils", d)
        return total

    image = images(gridded(0, frames), field_coef)
    return (image, field_coef)


def solution(mesh):
    placed = (
        P("frames", "coils", None, None, None),
        P("frames", None),
        P(),
        P(),
        P("coils", None, None, None),
        P("coils", None),
        P(None, "coils"),
        P(),
    )
    return jax.shard_map(
        local,
        mesh=mesh,
        in_specs=placed,
        out_specs=(P("frames", None, "coils", None), P("frames", None)),
        check_vma=False,
    )
```

```python
import functools
from jax._src.pallas.mosaic import core
import math

import jax
import jax.numpy as jnp
import ml_dtypes
import numpy as np
from jax import lax
from jax.experimental import pallas as pl
from jax.experimental.pallas import tpu as pltpu
from jax.sharding import PartitionSpec as P

BF16 = jnp.bfloat16
F32 = jnp.float32


def dft_tables(side):
    offsets = np.arange(side) - side // 2
    wrapped = np.mod(offsets[:, None] * offsets[None, :], side).astype(np.float32)
    phase = np.float32(2.0 * math.pi / side) * wrapped
    cosine = (np.cos(phase) / np.float32(side)).astype(ml_dtypes.bfloat16)
    sine = (np.sin(phase) / np.float32(side)).astype(ml_dtypes.bfloat16)
    right = np.block([[cosine, sine], [-sine, cosine]])
    left = np.block([[cosine, -sine], [sine, cosine]])
    return right, left


def windows(readout, segs):
    spacing, jitter = readout // segs, readout // (4 * segs)
    low = [0] + [j * spacing - jitter for j in range(1, segs)]
    high = [j * spacing + jitter for j in range(1, segs)] + [readout]
    width = 128
    while True:
        starts = [max(0, min(a // 16 * 16, readout - width)) for a in low]
        if all(s + width >= b for s, b in zip(starts, high)) or width >= readout:
            return starts, min(width, readout)
        width += 128


def edges_of(bounds_ref, readout, segs):
    return [0] + [bounds_ref[j] for j in range(segs - 1)] + [readout]


def centres(kdata_ref, center_ref):
    for t in range(kdata_ref.shape[0]):
        for c in range(kdata_ref.shape[1]):
            total = kdata_ref[t, c, 0].astype(F32)
            for s in range(1, kdata_ref.shape[2]):
                total += kdata_ref[t, c, s].astype(F32)
            center_ref[t, 0, c, :] = total[0]
            center_ref[t, 1, c, :] = total[1]


def drift(position_ref, center_ref, arrived_ref, first_ref, projection_ref, step_ref):
    frames, _, coils, lanes = center_ref.shape
    basis = projection_ref.shape[0]
    at_start = position_ref[0] == 0
    for t in range(frames):
        if t == 0:
            before = [jnp.where(at_start, first_ref[p], arrived_ref[p]) for p in range(2)]
        else:
            before = [center_ref[t - 1, p] for p in range(2)]
        now = [center_ref[t, p] for p in range(2)]
        cross = before[0] * now[1] - before[1] * now[0]
        energy = before[0] * before[0] + before[1] * before[1]
        energy = energy + (now[0] * now[0] + now[1] * now[1]) + 1.0
        signal = 2.0 * cross / energy
        for b in range(basis):
            row = jnp.sum(projection_ref[b] * signal, axis=0, keepdims=True)
            step_ref[pl.ds(t * basis + b, 1), :] = row


def grid_frames(starts, width, first, count, angles_ref, bounds_ref, kdata_ref, tables_ref, right_ref, left_ref, sens_ref, out_ref):
    _, coils, spokes, _, readout = kdata_ref.shape
    _, table, _, side = tables_ref.shape
    segs = len(starts)
    odd = spokes % 2
    padded = spokes + odd
    tiles = padded // 2
    pairs = coils // 2
    steps = count * pairs
    lanes = 128
    room = lanes // 4

    def body(kd, rows, turned, weighted, halves, ky, right, left, *accs):
        grid_acc = [accs[m * 8 : m * 8 + 3] for m in range(2)]
        half_acc = [accs[m * 8 + 3 : m * 8 + 5] for m in range(2)]
        image_acc = [accs[m * 8 + 5 : m * 8 + 8] for m in range(2)]
        edges = edges_of(bounds_ref, readout, segs)
        index = lax.broadcasted_iota(jnp.int32, (width, side), 0)

        def angle_tables(a, carry):
            ky[a] = tables_ref[1, a]
            for l in range(segs):
                at = index + starts[l]
                keep = (at >= edges[l]) & (at < edges[l + 1])
                part = jnp.where(keep, tables_ref[0, a, starts[l] : starts[l] + width, :].astype(F32), 0.0)
                rows[a, l] = part.T.astype(BF16)
            return carry

        lax.fori_loop(0, table, angle_tables, 0)
        right[...] = right_ref[...]
        left[...] = left_ref[...]
        out_ref[...] = jnp.zeros(out_ref.shape, F32)
        if odd:
            rows[table] = jnp.zeros((segs, side, width), BF16)
            weighted[:, :, :, spokes] = jnp.zeros((2, 2, 2, readout, side), BF16)

        def columns(i, carry):
            for s in range(spokes):
                for c in range(coils):
                    kd[c, 2 * s : 2 * s + 2, :] = kdata_ref[first + i, c, s].astype(F32)
            per = min(lanes // room, coils)
            for g in range(coils // per):
                flipped = kd[g * per : (g + 1) * per].reshape(per * room, readout).T
                for e in range(per):
                    turned[i, g * per + e, :, :room] = flipped[:, e * room : (e + 1) * room].astype(BF16)
            return carry

        lax.fori_loop(0, count, columns, 0)

        def place(step):
            return lax.div(step, pairs), lax.rem(step, pairs)

        def weigh(step, buf, m, s):
            i, n = place(step)
            column = turned[i, 2 * n + m, :, 2 * s : 2 * s + 2]
            factor = ky[angles_ref[first + i, s]]
            for p in range(2):
                scale = jnp.broadcast_to(column[:, p : p + 1], (readout, side))
                weighted[buf, m, p, s] = scale * factor

        def beside(blocks):
            return jnp.concatenate(blocks, axis=1)

        def grid_tile(step, buf, l, k):
            i, _ = place(step)
            spoke = [2 * k, 2 * k + 1]
            which = [angles_ref[first + i, s] if s < spokes else table for s in spoke]
            for m in range(2):
                rhs = beside([
                    weighted[buf, m, p, 2 * k : 2 * k + 2, starts[l] : starts[l] + width, :].reshape(2 * width, side)
                    for p in range(2)
                ])
                pltpu.matmul_push_rhs(rhs, k % 2, m)
            lhs = beside([rows[a, l] for a in which])
            for m in range(2):
                pltpu.matmul_acc_lhs(grid_acc[m][l], lhs, load_staged_rhs=k % 2)

        def over_columns(buf, l):
            for m in range(2):
                pltpu.matmul_push_rhs(beside([right[0], right[1]]), 1, m)
                gridded = pltpu.matmul_pop(grid_acc[m][l]).astype(BF16)
                pltpu.matmul_acc_lhs(half_acc[m][l % 2], gridded, load_staged_rhs=1)
            for m in range(2):
                half = pltpu.matmul_pop(half_acc[m][l % 2]).astype(BF16)
                halves[buf, m, l, 0] = half[:, :side]
                halves[buf, m, l, 1] = half[:, side:]

        def left_rows(h):
            return beside([left[q, h * side : (h + 1) * side] for q in range(2)])

        def over_rows_both(buf):
            for m in range(2):
                both = beside([halves[buf, m, l].reshape(2 * side, side) for l in range(2)])
                pltpu.matmul_push_rhs(both, 0, m)
            for h in range(2):
                for m in range(2):
                    pltpu.matmul_acc_lhs(image_acc[m][h], left_rows(h), load_staged_rhs=0 if h == 0 else None)

        def over_rows_last(buf):
            both = beside([halves[buf, m, 2].reshape(2 * side, side) for m in range(2)])
            for m in range(2):
                pltpu.matmul_push_rhs(both, 0, m)
                pltpu.matmul_acc_lhs(image_acc[m][2], left_rows(m), load_staged_rhs=0)

        def combine(step, l, parts):
            i, n = place(step)
            total_re, total_im = out_ref[i, l, 0], out_ref[i, l, 1]
            for m in range(2):
                re, im = parts[m]
                real = sens_ref[2 * n + m, 0].astype(F32)
                imag = sens_ref[2 * n + m, 1].astype(F32)
                total_re += real * re + imag * im
                total_im += real * im - imag * re
            out_ref[i, l, 0] = total_re
            out_ref[i, l, 1] = total_im

        def combine_both(step):
            images = [[pltpu.matmul_pop(image_acc[m][h]) for h in range(2)] for m in range(2)]
            for l in range(2):
                combine(step, l, [[part[:, l * side : (l + 1) * side] for part in images[m]] for m in range(2)])

        def combine_last(step):
            images = [pltpu.matmul_pop(image_acc[h][2]) for h in range(2)]
            combine(step, 2, [[part[:, m * side : (m + 1) * side] for part in images] for m in range(2)])

        def phase(step, buf, begin, end):
            ahead = [] if end else [(m, s) for s in range(spokes) for m in range(2)]
            chunks = [ahead[len(ahead) * n // (segs * tiles) : len(ahead) * (n + 1) // (segs * tiles)] for n in range(segs * tiles)]

            def grid_segment(l):
                for k in range(tiles):
                    for m, s in chunks[l * tiles + k]:
                        weigh(step + 1, 1 - buf, m, s)
                    grid_tile(step, buf, l, k)

            grid_segment(0)
            if not begin:
                over_columns(1 - buf, 2)
            grid_segment(1)
            over_columns(buf, 0)
            if not begin:
                over_rows_both(1 - buf)
            grid_segment(2)
            if not begin:
                over_rows_last(1 - buf)
                combine_both(step - 1)
            over_columns(buf, 1)
            if not begin:
                combine_last(step - 1)

        for s in range(spokes):
            for m in range(2):
                weigh(0, 0, m, s)
        phase(0, 0, True, False)

        def two(q, carry):
            phase(2 * q + 1, 1, False, False)
            phase(2 * q + 2, 0, False, False)
            return carry

        lax.fori_loop(0, steps // 2 - 1, two, 0)
        phase(steps - 1, 1, False, True)
        over_columns(1, 2)
        over_rows_both(1)
        over_rows_last(1)
        combine_both(steps - 1)
        combine_last(steps - 1)

    pl.run_scoped(
        body,
        pltpu.VMEM((coils, room, readout), F32),
        pltpu.VMEM((table + odd, segs, side, width), BF16),
        pltpu.VMEM((count, coils, readout, lanes), BF16),
        pltpu.VMEM((2, 2, 2, padded, readout, side), BF16),
        pltpu.VMEM((2, 2, segs, 2, side, side), BF16),
        pltpu.VMEM((table, readout, side), BF16),
        pltpu.VMEM((2, 2 * side, side), BF16),
        pltpu.VMEM((2, 2 * side, side), BF16),
        *[core.AccMemorySpace(m)((side, 2 * side), F32) for m in range(2) for _ in range(8)],
    )


def modulate(side, readout, position_ref, bounds_ref, coef_ref, parts_ref, *out_refs):
    frames, segs = parts_ref.shape[:2]
    owners = len(out_refs)
    rows = side // owners
    half = side // 2
    me = position_ref[0]
    edges = edges_of(bounds_ref, readout, segs)
    times = [(edges[l] + edges[l + 1] - 1).astype(F32) / (2.0 * readout) for l in range(segs)]
    lane = lax.broadcasted_iota(jnp.int32, (8, 128), 1)
    base = jnp.zeros((8, 128), F32)
    slope = jnp.zeros((8, 128), F32)
    scale = jnp.zeros((8, 128), F32)
    for t in range(frames):
        for l in range(segs):
            here = lane == t * segs + l
            base = jnp.where(here, coef_ref[t, 0], base)
            slope = jnp.where(here, coef_ref[t, 1], slope)
            scale = jnp.where(here, times[l], scale)
    down_pos = (lax.broadcasted_iota(jnp.int32, (side, 128), 0) - half).astype(F32) / half
    down = (base[:1] + slope[:1] * down_pos) * scale[:1]
    cos_down, sin_down = jnp.cos(down), jnp.sin(down)
    across_pos = (lax.broadcasted_iota(jnp.int32, (1, side), 1) - half).astype(F32) / half
    across = jnp.concatenate(
        [coef_ref[t, 2] * across_pos * times[l] for t in range(frames) for l in range(segs)], axis=0
    )
    cos_across, sin_across = jnp.cos(across), jnp.sin(across)
    for t in range(frames):
        image_re = jnp.zeros((side, side), F32)
        image_im = jnp.zeros((side, side), F32)
        for l in range(segs):
            n = t * segs + l
            cr, sr = cos_down[:, n : n + 1], sin_down[:, n : n + 1]
            cc, sc = cos_across[n : n + 1], sin_across[n : n + 1]
            cos = cr * cc - sr * sc
            sin = sr * cc + cr * sc
            re, im = parts_ref[t, l, 0], parts_ref[t, l, 1]
            image_re += cos * re - sin * im
            image_im += sin * re + cos * im
        for owner in range(owners):
            for d, out_ref in enumerate(out_refs):

                @pl.when(lax.rem(me + d, owners) == owner)
                def _():
                    out_ref[t, 0] = image_re[owner * rows : (owner + 1) * rows]
                    out_ref[t, 1] = image_im[owner * rows : (owner + 1) * rows]


def shifted(block, axis, distance):
    count = lax.axis_size(axis)
    return lax.ppermute(block, axis, [(i, i + distance) for i in range(count - distance)])


def around(block, axis, distance):
    count = lax.axis_size(axis)
    return lax.ppermute(block, axis, [(i, (i + distance) % count) for i in range(count)])


def exchanged(block, axis, distance):
    return lax.ppermute(block, axis, [(i, i ^ distance) for i in range(lax.axis_size(axis))])


def local(kdata, angles, kernels, seg_bounds, sensitivity, ref_center, projection, init_coef):
    frames, coils, _, spokes, readout = kdata.shape
    side = kernels.shape[3]
    segs = seg_bounds.shape[0] + 1
    basis = projection.shape[0]
    owners = lax.axis_size("coils")
    starts, width = windows(readout, segs)
    right, left = (jnp.stack(jnp.split(jnp.asarray(table), 2, axis=1)) for table in dft_tables(side))
    kd = jnp.swapaxes(kdata, 2, 3)
    smem = pl.BlockSpec(memory_space=pltpu.SMEM)
    vmem = pl.BlockSpec(memory_space=pltpu.VMEM)
    place = lax.axis_index("frames").astype(jnp.int32)
    owner = lax.axis_index("coils").astype(jnp.int32)

    lanes = 128
    center = pl.pallas_call(
        centres,
        grid=(1,),
        out_shape=jax.ShapeDtypeStruct((frames, 2, coils, lanes), F32),
        in_specs=[pl.BlockSpec((frames, coils, spokes, 2, lanes), lambda i: (0, 0, 0, 0, readout // 2 // lanes))],
        out_specs=pl.BlockSpec((frames, 2, coils, lanes), lambda i: (0, 0, 0, 0)),
        name="centres",
    )(kd)

    arrived = shifted(center[-1], "frames", 1)
    first = jnp.broadcast_to(ref_center.T[:, :, None], (2, coils, lanes))
    weights = jnp.broadcast_to(projection[:, :, None], (basis, coils, lanes))
    step = pl.pallas_call(
        drift,
        out_shape=jax.ShapeDtypeStruct((frames * basis, lanes), F32),
        in_specs=[smem, vmem, vmem, vmem, vmem],
        out_specs=vmem,
        name="drift",
    )(place.reshape(1), center, arrived, first, weights)
    increment = step[:, :1].reshape(frames, basis)
    distance = 1
    while distance < owners:
        increment = increment + exchanged(increment, "coils", distance)
        distance *= 2
    running = jnp.sum(increment, axis=0)
    before = jnp.zeros_like(running)
    distance = 1
    while distance < lax.axis_size("frames"):
        came = exchanged(running, "frames", distance)
        before = before + jnp.where((place & distance) != 0, came, 0.0)
        running = running + came
        distance *= 2
    field_coef = init_coef[None, :] + (before[None, :] + jnp.cumsum(increment, axis=0))

    parts = pl.pallas_call(
        functools.partial(grid_frames, starts, width, 0, frames),
        out_shape=jax.ShapeDtypeStruct((frames, segs, 2, side, side), F32),
        in_specs=[smem, smem, vmem, vmem, vmem, vmem, vmem],
        out_specs=vmem,
        name="gridding",
    )(angles, seg_bounds, kd, kernels, right, left, sensitivity)

    block = jax.ShapeDtypeStruct((frames, 2, side // owners, side), F32)
    blocks = pl.pallas_call(
        functools.partial(modulate, side, readout),
        out_shape=(block,) * owners,
        in_specs=[smem, smem, smem, vmem],
        out_specs=(vmem,) * owners,
        name="modulate",
    )(owner.reshape(1), seg_bounds, field_coef, parts)
    image = blocks[0]
    for d in range(1, owners):
        image = image + around(blocks[d], "coils", d)
    return (image, field_coef)


def solution(mesh):
    placed = (
        P("frames", "coils", None, None, None),
        P("frames", None),
        P(),
        P(),
        P("coils", None, None, None),
        P("coils", None),
        P(None, "coils"),
        P(),
    )
    def located(*arguments):
        with jax.sharding.use_abstract_mesh(mesh.abstract_mesh):
            return local(*arguments)

    return jax.shard_map(
        local,
        mesh=mesh,
        in_specs=placed,
        out_specs=(P("frames", None, "coils", None), P("frames", None)),
        check_vma=False,
    )
```

```python
import functools
from jax._src.pallas.mosaic import core
import math

import jax
import jax.numpy as jnp
import ml_dtypes
import numpy as np
from jax import lax
from jax.experimental import pallas as pl
from jax.experimental.pallas import tpu as pltpu
from jax.sharding import PartitionSpec as P

BF16 = jnp.bfloat16
F32 = jnp.float32


def dft_tables(side):
    offsets = np.arange(side) - side // 2
    wrapped = np.mod(offsets[:, None] * offsets[None, :], side).astype(np.float32)
    phase = np.float32(2.0 * math.pi / side) * wrapped
    cosine = (np.cos(phase) / np.float32(side)).astype(ml_dtypes.bfloat16)
    sine = (np.sin(phase) / np.float32(side)).astype(ml_dtypes.bfloat16)
    right = np.block([[cosine, sine], [-sine, cosine]])
    left = np.block([[cosine, -sine], [sine, cosine]])
    return right, left


def windows(readout, segs):
    spacing, jitter = readout // segs, readout // (4 * segs)
    low = [0] + [j * spacing - jitter for j in range(1, segs)]
    high = [j * spacing + jitter for j in range(1, segs)] + [readout]
    width = 128
    while True:
        starts = [max(0, min(a // 16 * 16, readout - width)) for a in low]
        if all(s + width >= b for s, b in zip(starts, high)) or width >= readout:
            return starts, min(width, readout)
        width += 128


def edges_of(bounds_ref, readout, segs):
    return [0] + [bounds_ref[j] for j in range(segs - 1)] + [readout]


def centres(kdata_ref, center_ref, last_ref):
    frames, coils = kdata_ref.shape[:2]
    for t in range(frames):
        for c in range(coils):
            total = kdata_ref[t, c, 0].astype(F32)
            for s in range(1, kdata_ref.shape[2]):
                total += kdata_ref[t, c, s].astype(F32)
            for p in range(2):
                center_ref[t, p, c, :] = total[p]
                if t == frames - 1:
                    last_ref[p, c, :] = total[p]


def drift(position_ref, projection_ref, center_ref, arrived_ref, first_ref, step_ref):
    frames, _, coils, lanes = center_ref.shape
    basis = projection_ref.shape[0]
    at_start = position_ref[0] == 0
    row = lax.broadcasted_iota(jnp.int32, (coils, lanes), 0)
    weights = []
    for b in range(basis):
        weight = jnp.zeros((coils, lanes), F32)
        for c in range(coils):
            weight = jnp.where(row == c, projection_ref[b, c], weight)
        weights.append(weight)
    step_ref[...] = jnp.zeros(step_ref.shape, F32)
    totals = [jnp.zeros((1, lanes), F32)] * basis
    for t in range(frames):
        if t == 0:
            before = [
                jnp.where(at_start, jnp.broadcast_to(first_ref[:, p : p + 1], (coils, lanes)), arrived_ref[p])
                for p in range(2)
            ]
        else:
            before = [center_ref[t - 1, p] for p in range(2)]
        now = [center_ref[t, p] for p in range(2)]
        cross = before[0] * now[1] - before[1] * now[0]
        energy = before[0] * before[0] + before[1] * before[1]
        energy = energy + (now[0] * now[0] + now[1] * now[1]) + 1.0
        signal = 2.0 * cross / energy
        for b in range(basis):
            part = jnp.sum(weights[b] * signal, axis=0, keepdims=True)
            step_ref[pl.ds(t * basis + b, 1), :] = part
            totals[b] = totals[b] + part
    for b in range(basis):
        step_ref[pl.ds(frames * basis + b, 1), :] = totals[b]


def grid_frames(starts, width, first, count, angles_ref, bounds_ref, kdata_ref, tables_ref, right_ref, left_ref, sens_ref, out_ref):
    _, coils, spokes, _, readout = kdata_ref.shape
    _, table, _, side = tables_ref.shape
    segs = len(starts)
    most = (spokes + 1) // 2
    least = min(3, most)
    pairs = coils // 2
    steps = count * pairs
    lanes = 128
    room = max(8, 2 * coils)
    group = lanes // room
    groups = (2 * most + group - 1) // group
    cut = 32
    cuts = side // cut

    def body(kd, flipped, columns, rows, weighted, halves, ky, right, left, slot_of, angle_of, tiles_of, *accs):
        banks = [[accs[(m * 8 + b) * cuts : (m * 8 + b + 1) * cuts] for b in range(8)] for m in range(2)]
        grid_acc = [banks[m][:3] for m in range(2)]
        half_acc = [banks[m][3:5] for m in range(2)]
        image_acc = [banks[m][5:] for m in range(2)]

        def multiply(bank, lhs, staged):
            for r in range(cuts):
                pltpu.matmul_acc_lhs(bank[r], lhs[r * cut : (r + 1) * cut], load_staged_rhs=None if r else staged)
        edges = edges_of(bounds_ref, readout, segs)
        index = lax.broadcasted_iota(jnp.int32, (width, side), 0)
        keep = []
        for l in range(segs):
            at = index + starts[l]
            keep.append(jnp.where((at >= edges[l]) & (at < edges[l + 1]), 1.0, 0.0).astype(BF16))

        def angle_tables(a, carry):
            ky[a] = tables_ref[1, a]
            for l in range(segs):
                rows[a, l] = (tables_ref[0, a, starts[l] : starts[l] + width, :] * keep[l]).T
            return carry

        lax.fori_loop(0, table, angle_tables, 0)
        ky[table] = jnp.zeros((readout, side), BF16)
        rows[table] = jnp.zeros((segs, side, width), BF16)
        right[...] = right_ref[...]
        left[...] = left_ref[...]
        halves[...] = jnp.zeros(halves.shape, BF16)
        out_ref[...] = jnp.zeros(out_ref.shape, F32)

        def gather(i, carry):
            kd[...] = jnp.zeros(kd.shape, F32)
            for a in range(table):
                slot_of[a] = -1
            for n in range(2 * most):
                angle_of[i, n] = table
            used = jnp.int32(0)
            for s in range(spokes):
                a = angles_ref[first + i, s]
                old = slot_of[a]
                slot = jnp.where(old < 0, used, old)
                used = used + jnp.where(old < 0, 1, 0)
                slot_of[a] = slot
                angle_of[i, slot] = a
                for c in range(coils):
                    kd[slot, 2 * c : 2 * c + 2, :] += kdata_ref[first + i, c, s].astype(F32)
            tiles_of[i] = jnp.maximum(lax.div(used + 1, 2), least)
            for g in range(groups):
                flipped[i, g] = kd[g * group : (g + 1) * group].reshape(lanes, readout).T
            return carry

        lax.fori_loop(0, count, gather, 0)

        def place(step):
            return lax.div(step, pairs), lax.rem(step, pairs)

        def own_columns(step):
            i, n = place(step)
            for g in range(groups):
                columns[g] = pltpu.roll(flipped[i, g], lanes - 4 * n, 1).astype(BF16)

        def weigh(step, k, buf):
            i, _ = place(step)
            for e in range(2):
                slot = 2 * k + e
                factor = ky[angle_of[i, slot]]
                for m in range(2):
                    for p in range(2):
                        lane = slot % group * room + 2 * m + p
                        column = columns[slot // group, :, lane : lane + 1]
                        weighted[buf, m, p, e] = jnp.broadcast_to(column, (readout, side)) * factor

        def beside(blocks):
            return jnp.concatenate(blocks, axis=1)

        def grid_tile(step, buf, l, k):
            i, _ = place(step)
            for m in range(2):
                rhs = beside([
                    weighted[buf, m, p, :, starts[l] : starts[l] + width, :].reshape(2 * width, side) for p in range(2)
                ])
                pltpu.matmul_push_rhs(rhs, l % 2, m)
            lhs = beside([rows[angle_of[i, 2 * k + e], l] for e in range(2)])
            for m in range(2):
                multiply(grid_acc[m][l], lhs, l % 2)

        def over_columns(l):
            for m in range(2):
                pltpu.matmul_push_rhs(beside([right[0], right[1]]), 1, m)
            for r in range(cuts):
                for m in range(2):
                    gridded = pltpu.matmul_pop(grid_acc[m][l][r]).astype(BF16)
                    pltpu.matmul_acc_lhs(half_acc[m][l % 2][r], gridded, load_staged_rhs=None if r else 1)

        def keep_half(l):
            for r in range(cuts):
                for m in range(2):
                    half = pltpu.matmul_pop(half_acc[m][l % 2][r]).astype(BF16)
                    halves[m, l, 0, r * cut : (r + 1) * cut] = half[:, :side]
                    halves[m, l, 1, r * cut : (r + 1) * cut] = half[:, side:]

        def left_rows(h):
            return beside([left[q, h * side : (h + 1) * side] for q in range(2)])

        def over_rows():
            for m in range(2):
                both = beside([halves[m, l].reshape(2 * side, side) for l in range(2)])
                pltpu.matmul_push_rhs(both, 0, m)
            last = beside([halves[m, 2].reshape(2 * side, side) for m in range(2)])
            for m in range(2):
                pltpu.matmul_push_rhs(last, 1, m)
            for h in range(2):
                for m in range(2):
                    multiply(image_acc[m][h], left_rows(h), 0 if h == 0 else None)
            for m in range(2):
                multiply(image_acc[m][2], left_rows(m), 1)

        def combine(step, r):
            i, n = place(step)
            here = pl.ds(r * cut, cut)
            real = [sens_ref[2 * n + m, 0, here].astype(F32) for m in range(2)]
            imag = [sens_ref[2 * n + m, 1, here].astype(F32) for m in range(2)]

            def add(l, parts):
                total_re, total_im = out_ref[i, l, 0, here], out_ref[i, l, 1, here]
                for m in range(2):
                    re, im = parts[m]
                    total_re += real[m] * re + imag[m] * im
                    total_im += real[m] * im - imag[m] * re
                out_ref[i, l, 0, here] = total_re
                out_ref[i, l, 1, here] = total_im

            images = [[pltpu.matmul_pop(image_acc[m][h][r]) for h in range(2)] for m in range(2)]
            for l in range(2):
                add(l, [[part[:, l * side : (l + 1) * side] for part in images[m]] for m in range(2)])
            images = [pltpu.matmul_pop(image_acc[h][2][r]) for h in range(2)]
            add(2, [[part[:, m * side : (m + 1) * side] for part in images] for m in range(2)])

        def phase(tiles, step):
            earlier = jnp.maximum(step - 1, 0)
            following = jnp.minimum(step + 1, steps - 1)
            left_over = list(range(cuts))
            for k in range(tiles):
                buf = k % 2 if k else 2
                last = k == tiles - 1
                if last:
                    weigh(following, 0, 2)
                else:
                    weigh(step, k + 1, (k + 1) % 2)
                for l in range(segs):
                    grid_tile(step, buf, l, k)
                    if k == 0 and l < 2:
                        over_columns(l + 1)
                    if k >= 2 and (l or k > 2) and left_over:
                        combine(earlier, left_over.pop(0))
                    if k == tiles - 2 and l == 1:
                        own_columns(following)
                    if last and l == 1:
                        over_columns(0)
                if k == 0:
                    keep_half(1)
                    keep_half(2)
                if k == 1:
                    over_rows()
            keep_half(0)
            for r in left_over:
                combine(earlier, r)

        own_columns(0)
        weigh(0, 0, 2)

        def one(step, carry):
            i, _ = place(step)
            tiles = tiles_of[i]
            for option in range(least, most + 1):
                pl.when(tiles == option)(functools.partial(phase, option, step))
            return carry

        lax.fori_loop(0, steps, one, 0)
        over_columns(1)
        over_columns(2)
        keep_half(1)
        keep_half(2)
        over_rows()
        for r in range(cuts):
            combine(steps - 1, r)

    pl.run_scoped(
        body,
        pltpu.VMEM((groups * group, room, readout), F32),
        pltpu.VMEM((count, groups, readout, lanes), F32),
        pltpu.VMEM((groups, readout, lanes), BF16),
        pltpu.VMEM((table + 1, segs, side, width), BF16),
        pltpu.VMEM((3, 2, 2, 2, readout, side), BF16),
        pltpu.VMEM((2, segs, 2, side, side), BF16),
        pltpu.VMEM((table + 1, readout, side), BF16),
        pltpu.VMEM((2, 2 * side, side), BF16),
        pltpu.VMEM((2, 2 * side, side), BF16),
        pltpu.SMEM((table,), jnp.int32),
        pltpu.SMEM((count, 2 * most), jnp.int32),
        pltpu.SMEM((count,), jnp.int32),
        *[core.AccMemorySpace(m)((cut, 2 * side), F32) for m in range(2) for _ in range(8 * cuts)],
    )


def modulate(
    readout, position_ref, bounds_ref, init_ref, increment_ref, before_ref, parts_ref, coef_ref, *refs
):
    *out_refs, image_ref = refs
    frames, segs, _, side, _ = parts_ref.shape
    basis = init_ref.shape[0]
    owners = len(out_refs)
    rows = side // owners
    half = side // 2
    me = position_ref[0]
    edges = edges_of(bounds_ref, readout, segs)
    times = [(edges[l] + edges[l + 1] - 1).astype(F32) / (2.0 * readout) for l in range(segs)]
    running = [before_ref[pl.ds(frames * basis + b, 1), :1] for b in range(basis)]
    coef = []
    for t in range(frames):
        for b in range(basis):
            running[b] = running[b] + increment_ref[pl.ds(t * basis + b, 1), :1]
            value = init_ref[b] + running[b]
            coef.append(value)
            coef_ref[pl.ds(t * basis + b, 1), :] = jnp.broadcast_to(value, (1, coef_ref.shape[1]))
    lane = lax.broadcasted_iota(jnp.int32, (1, 128), 1)
    base = jnp.zeros((1, 128), F32)
    slope = jnp.zeros((1, 128), F32)
    scale = jnp.zeros((1, 128), F32)
    for t in range(frames):
        for l in range(segs):
            here = lane == t * segs + l
            base = jnp.where(here, coef[t * basis], base)
            slope = jnp.where(here, coef[t * basis + 1], slope)
            scale = jnp.where(here, times[l], scale)
    down_pos = (lax.broadcasted_iota(jnp.int32, (side, 128), 0) - half).astype(F32) / half
    down = (base + slope * down_pos) * scale
    cos_down, sin_down = jnp.cos(down), jnp.sin(down)
    across_pos = (lax.broadcasted_iota(jnp.int32, (1, side), 1) - half).astype(F32) / half
    across = jnp.concatenate(
        [coef[t * basis + 2] * across_pos * times[l] for t in range(frames) for l in range(segs)], axis=0
    )
    cos_across, sin_across = jnp.cos(across), jnp.sin(across)
    for t in range(frames):
        image_re = jnp.zeros((side, side), F32)
        image_im = jnp.zeros((side, side), F32)
        for l in range(segs):
            n = t * segs + l
            cr, sr = cos_down[:, n : n + 1], sin_down[:, n : n + 1]
            cc, sc = cos_across[n : n + 1], sin_across[n : n + 1]
            cos = cr * cc - sr * sc
            sin = sr * cc + cr * sc
            re, im = parts_ref[t, l, 0], parts_ref[t, l, 1]
            image_re += cos * re - sin * im
            image_im += sin * re + cos * im
        image_ref[0] = image_re
        image_ref[1] = image_im
        for d, out_ref in enumerate(out_refs):
            owned = pl.multiple_of(lax.rem(me + d, owners) * rows, rows)
            out_ref[t] = image_ref[:, pl.ds(owned, rows), :]


def shifted(block, axis, distance):
    count = lax.axis_size(axis)
    return lax.ppermute(block, axis, [(i, i + distance) for i in range(count - distance)])


def around(block, axis, distance):
    count = lax.axis_size(axis)
    return lax.ppermute(block, axis, [(i, (i + distance) % count) for i in range(count)])


def exchanged(block, axis, distance):
    return lax.ppermute(block, axis, [(i, i ^ distance) for i in range(lax.axis_size(axis))])


def local(kdata, angles, kernels, seg_bounds, sensitivity, ref_center, projection, init_coef):
    frames, coils, _, spokes, readout = kdata.shape
    side = kernels.shape[3]
    segs = seg_bounds.shape[0] + 1
    basis = projection.shape[0]
    owners = lax.axis_size("coils")
    starts, width = windows(readout, segs)
    right, left = (jnp.stack(jnp.split(jnp.asarray(table), 2, axis=1)) for table in dft_tables(side))
    kd = jnp.swapaxes(kdata, 2, 3)
    smem = pl.BlockSpec(memory_space=pltpu.SMEM)
    vmem = pl.BlockSpec(memory_space=pltpu.VMEM)
    place = lax.axis_index("frames").astype(jnp.int32)
    owner = lax.axis_index("coils").astype(jnp.int32)

    lanes = 128
    center, last = pl.pallas_call(
        centres,
        grid=(1,),
        out_shape=(
            jax.ShapeDtypeStruct((frames, 2, coils, lanes), F32),
            jax.ShapeDtypeStruct((2, coils, lanes), F32),
        ),
        in_specs=[pl.BlockSpec((frames, coils, spokes, 2, lanes), lambda i: (0, 0, 0, 0, readout // 2 // lanes))],
        out_specs=(
            pl.BlockSpec((frames, 2, coils, lanes), lambda i: (0, 0, 0, 0)),
            pl.BlockSpec((2, coils, lanes), lambda i: (0, 0, 0)),
        ),
        name="centres",
    )(kd)
    arrived = shifted(last, "frames", 1)
    padded = ((frames + 1) * basis + 7) // 8 * 8
    increment = pl.pallas_call(
        drift,
        out_shape=jax.ShapeDtypeStruct((padded, lanes), F32),
        in_specs=[smem, smem, vmem, vmem, vmem],
        out_specs=vmem,
        name="drift",
    )(place.reshape(1), projection, center, arrived, ref_center)
    distance = 1
    while distance < owners:
        increment = increment + exchanged(increment, "coils", distance)
        distance *= 2
    running = increment
    before = jnp.zeros_like(running)
    distance = 1
    while distance < lax.axis_size("frames"):
        came = exchanged(running, "frames", distance)
        before = before + jnp.where((place & distance) != 0, came, 0.0)
        running = running + came
        distance *= 2

    parts = pl.pallas_call(
        functools.partial(grid_frames, starts, width, 0, frames),
        out_shape=jax.ShapeDtypeStruct((frames, segs, 2, side, side), F32),
        in_specs=[smem, smem, vmem, vmem, vmem, vmem, vmem],
        out_specs=vmem,
        name="gridding",
    )(angles, seg_bounds, kd, kernels, right, left, sensitivity)

    block = jax.ShapeDtypeStruct((frames, 2, side // owners, side), F32)
    coef, *blocks = pl.pallas_call(
        functools.partial(modulate, readout),
        out_shape=(jax.ShapeDtypeStruct((padded, lanes), F32),) + (block,) * owners,
        in_specs=[smem, smem, smem, vmem, vmem, vmem],
        out_specs=(vmem,) * (1 + owners),
        scratch_shapes=[pltpu.VMEM((2, side, side), F32)],
        name="modulate",
    )(owner.reshape(1), seg_bounds, init_coef, increment, before, parts)
    image = blocks[0]
    for d in range(1, owners):
        image = image + around(blocks[d], "coils", d)
    field_coef = coef[: frames * basis, 0].reshape(frames, basis)
    return (image, field_coef)


def solution(mesh):
    placed = (
        P("frames", "coils", None, None, None),
        P("frames", None),
        P(),
        P(),
        P("coils", None, None, None),
        P("coils", None),
        P(None, "coils"),
        P(),
    )
    def located(*arguments):
        with jax.sharding.use_abstract_mesh(mesh.abstract_mesh):
            return local(*arguments)

    return jax.shard_map(
        local,
        mesh=mesh,
        in_specs=placed,
        out_specs=(P("frames", None, "coils", None), P("frames", None)),
        check_vma=False,
    )
```

```python
import functools
from jax._src.pallas.mosaic import core
import math

import jax
import jax.numpy as jnp
import ml_dtypes
import numpy as np
from jax import lax
from jax.experimental import pallas as pl
from jax.experimental.pallas import tpu as pltpu
from jax.sharding import PartitionSpec as P

BF16 = jnp.bfloat16
F32 = jnp.float32


def dft_tables(side):
    offsets = np.arange(side) - side // 2
    wrapped = np.mod(offsets[:, None] * offsets[None, :], side).astype(np.float32)
    phase = np.float32(2.0 * math.pi / side) * wrapped
    cosine = (np.cos(phase) / np.float32(side)).astype(ml_dtypes.bfloat16)
    sine = (np.sin(phase) / np.float32(side)).astype(ml_dtypes.bfloat16)
    right = np.block([[cosine, sine], [-sine, cosine]])
    left = np.block([[cosine, -sine], [sine, cosine]])
    return right, left


def windows(readout, segs):
    spacing, jitter = readout // segs, readout // (4 * segs)
    low = [0] + [j * spacing - jitter for j in range(1, segs)]
    high = [j * spacing + jitter for j in range(1, segs)] + [readout]
    width = 128
    while True:
        starts = [max(0, min(a // 16 * 16, readout - width)) for a in low]
        if all(s + width >= b for s, b in zip(starts, high)) or width >= readout:
            return starts, min(width, readout)
        width += 128


def edges_of(bounds_ref, readout, segs):
    return [0] + [bounds_ref[j] for j in range(segs - 1)] + [readout]


def centres(kdata_ref, first_ref, projection_ref, block_ref, center_ref):
    frames, coils = kdata_ref.shape[:2]
    rows, lanes = block_ref.shape
    basis = projection_ref.shape[0]
    lane = lax.broadcasted_iota(jnp.int32, (rows, lanes), 1)
    row = lax.broadcasted_iota(jnp.int32, (rows, lanes), 0)
    if rows > coils:
        center_ref[...] = jnp.zeros(center_ref.shape, F32)
    for t in range(frames):
        for c in range(coils):
            total = kdata_ref[t, c, 0].astype(F32)
            for s in range(1, kdata_ref.shape[2]):
                total += kdata_ref[t, c, s].astype(F32)
            for p in range(2):
                center_ref[2 * t + p, c, :] = total[p]
    block = jnp.zeros((rows, lanes), F32)
    for c in range(coils):
        values = [first_ref[p, c] for p in range(2)] + [projection_ref[b, c] for b in range(basis)]
        for n, value in enumerate(values):
            block = jnp.where((row == c) & (lane == 2 * frames + n), value, block)
    for n in range(2 * frames):
        block = jnp.where(lane == n, jnp.broadcast_to(center_ref[n][:, :1], (rows, lanes)), block)
    block_ref[...] = block


def grid_frames(starts, width, first, count, angles_ref, bounds_ref, kdata_ref, tables_ref, right_ref, left_ref, sens_ref, out_ref):
    _, coils, spokes, _, readout = kdata_ref.shape
    _, table, _, side = tables_ref.shape
    segs = len(starts)
    most = (spokes + 1) // 2
    least = min(3, most)
    pairs = coils // 2
    steps = count * pairs
    lanes = 128
    room = max(8, 2 * coils)
    group = lanes // room
    groups = (2 * most + group - 1) // group
    cut = 32
    cuts = side // cut

    def body(kd, flipped, columns, rows, weighted, halves, ky, right, left, slot_of, angle_of, tiles_of, *accs):
        banks = [[accs[(m * 8 + b) * cuts : (m * 8 + b + 1) * cuts] for b in range(8)] for m in range(2)]
        grid_acc = [banks[m][:3] for m in range(2)]
        half_acc = [banks[m][3:5] for m in range(2)]
        image_acc = [banks[m][5:] for m in range(2)]

        def multiply(bank, lhs, staged):
            for r in range(cuts):
                pltpu.matmul_acc_lhs(bank[r], lhs[r * cut : (r + 1) * cut], load_staged_rhs=None if r else staged)
        edges = edges_of(bounds_ref, readout, segs)
        index = lax.broadcasted_iota(jnp.int32, (width, side), 0)
        keep = []
        for l in range(segs):
            at = index + starts[l]
            keep.append(jnp.where((at >= edges[l]) & (at < edges[l + 1]), 1.0, 0.0).astype(BF16))

        def angle_tables(a, carry):
            ky[a] = tables_ref[1, a]
            for l in range(segs):
                rows[a, l] = (tables_ref[0, a, starts[l] : starts[l] + width, :] * keep[l]).T
            return carry

        lax.fori_loop(0, table, angle_tables, 0)
        ky[table] = jnp.zeros((readout, side), BF16)
        rows[table] = jnp.zeros((segs, side, width), BF16)
        right[...] = right_ref[...]
        left[...] = left_ref[...]
        halves[...] = jnp.zeros(halves.shape, BF16)
        out_ref[...] = jnp.zeros(out_ref.shape, F32)

        def gather(i, carry):
            kd[...] = jnp.zeros(kd.shape, F32)
            for a in range(table):
                slot_of[a] = -1
            for n in range(2 * most):
                angle_of[i, n] = table
            used = jnp.int32(0)
            for s in range(spokes):
                a = angles_ref[first + i, s]
                old = slot_of[a]
                slot = jnp.where(old < 0, used, old)
                used = used + jnp.where(old < 0, 1, 0)
                slot_of[a] = slot
                angle_of[i, slot] = a
                for c in range(coils):
                    kd[slot, 2 * c : 2 * c + 2, :] += kdata_ref[first + i, c, s].astype(F32)
            tiles_of[i] = jnp.maximum(lax.div(used + 1, 2), least)
            for g in range(groups):
                flipped[i, g] = kd[g * group : (g + 1) * group].reshape(lanes, readout).T
            return carry

        lax.fori_loop(0, count, gather, 0)

        def place(step):
            return lax.div(step, pairs), lax.rem(step, pairs)

        def own_columns(step):
            i, n = place(step)
            for g in range(groups):
                columns[g] = pltpu.roll(flipped[i, g], lanes - 4 * n, 1).astype(BF16)

        def weigh(step, k, buf):
            i, _ = place(step)
            for e in range(2):
                slot = 2 * k + e
                factor = ky[angle_of[i, slot]]
                for m in range(2):
                    for p in range(2):
                        lane = slot % group * room + 2 * m + p
                        column = columns[slot // group, :, lane : lane + 1]
                        weighted[buf, m, p, e] = jnp.broadcast_to(column, (readout, side)) * factor

        def beside(blocks):
            return jnp.concatenate(blocks, axis=1)

        def grid_tile(step, buf, l, k):
            i, _ = place(step)
            for m in range(2):
                rhs = beside([
                    weighted[buf, m, p, :, starts[l] : starts[l] + width, :].reshape(2 * width, side) for p in range(2)
                ])
                pltpu.matmul_push_rhs(rhs, l % 2, m)
            lhs = beside([rows[angle_of[i, 2 * k + e], l] for e in range(2)])
            for m in range(2):
                multiply(grid_acc[m][l], lhs, l % 2)

        def over_columns(l):
            for m in range(2):
                pltpu.matmul_push_rhs(beside([right[0], right[1]]), 1, m)
            for r in range(cuts):
                for m in range(2):
                    gridded = pltpu.matmul_pop(grid_acc[m][l][r]).astype(BF16)
                    pltpu.matmul_acc_lhs(half_acc[m][l % 2][r], gridded, load_staged_rhs=None if r else 1)

        def keep_half(l):
            for r in range(cuts):
                for m in range(2):
                    half = pltpu.matmul_pop(half_acc[m][l % 2][r]).astype(BF16)
                    halves[m, l, 0, r * cut : (r + 1) * cut] = half[:, :side]
                    halves[m, l, 1, r * cut : (r + 1) * cut] = half[:, side:]

        def left_rows(h):
            return beside([left[q, h * side : (h + 1) * side] for q in range(2)])

        def over_rows():
            for m in range(2):
                both = beside([halves[m, l].reshape(2 * side, side) for l in range(2)])
                pltpu.matmul_push_rhs(both, 0, m)
            last = beside([halves[m, 2].reshape(2 * side, side) for m in range(2)])
            for m in range(2):
                pltpu.matmul_push_rhs(last, 1, m)
            for h in range(2):
                for m in range(2):
                    multiply(image_acc[m][h], left_rows(h), 0 if h == 0 else None)
            for m in range(2):
                multiply(image_acc[m][2], left_rows(m), 1)

        def combine(step, r):
            i, n = place(step)
            here = pl.ds(r * cut, cut)
            real = [sens_ref[2 * n + m, 0, here].astype(F32) for m in range(2)]
            imag = [sens_ref[2 * n + m, 1, here].astype(F32) for m in range(2)]

            def add(l, parts):
                total_re, total_im = out_ref[i, l, 0, here], out_ref[i, l, 1, here]
                for m in range(2):
                    re, im = parts[m]
                    total_re += real[m] * re + imag[m] * im
                    total_im += real[m] * im - imag[m] * re
                out_ref[i, l, 0, here] = total_re
                out_ref[i, l, 1, here] = total_im

            images = [[pltpu.matmul_pop(image_acc[m][h][r]) for h in range(2)] for m in range(2)]
            for l in range(2):
                add(l, [[part[:, l * side : (l + 1) * side] for part in images[m]] for m in range(2)])
            images = [pltpu.matmul_pop(image_acc[h][2][r]) for h in range(2)]
            add(2, [[part[:, m * side : (m + 1) * side] for part in images] for m in range(2)])

        def phase(tiles, step):
            earlier = jnp.maximum(step - 1, 0)
            following = jnp.minimum(step + 1, steps - 1)
            left_over = list(range(cuts))
            for k in range(tiles):
                buf = k % 2 if k else 2
                last = k == tiles - 1
                if last:
                    weigh(following, 0, 2)
                else:
                    weigh(step, k + 1, (k + 1) % 2)
                for l in range(segs):
                    grid_tile(step, buf, l, k)
                    if k == 0 and l < 2:
                        over_columns(l + 1)
                    if k >= 2 and (l or k > 2) and left_over:
                        combine(earlier, left_over.pop(0))
                    if k == tiles - 2 and l == 1:
                        own_columns(following)
                    if last and l == 1:
                        over_columns(0)
                if k == 0:
                    keep_half(1)
                    keep_half(2)
                if k == 1:
                    over_rows()
            keep_half(0)
            for r in left_over:
                combine(earlier, r)

        own_columns(0)
        weigh(0, 0, 2)

        def one(step, carry):
            i, _ = place(step)
            tiles = tiles_of[i]
            for option in range(least, most + 1):
                pl.when(tiles == option)(functools.partial(phase, option, step))
            return carry

        lax.fori_loop(0, steps, one, 0)
        over_columns(1)
        over_columns(2)
        keep_half(1)
        keep_half(2)
        over_rows()
        for r in range(cuts):
            combine(steps - 1, r)

    pl.run_scoped(
        body,
        pltpu.VMEM((groups * group, room, readout), F32),
        pltpu.VMEM((count, groups, readout, lanes), F32),
        pltpu.VMEM((groups, readout, lanes), BF16),
        pltpu.VMEM((table + 1, segs, side, width), BF16),
        pltpu.VMEM((3, 2, 2, 2, readout, side), BF16),
        pltpu.VMEM((2, segs, 2, side, side), BF16),
        pltpu.VMEM((table + 1, readout, side), BF16),
        pltpu.VMEM((2, 2 * side, side), BF16),
        pltpu.VMEM((2, 2 * side, side), BF16),
        pltpu.SMEM((table,), jnp.int32),
        pltpu.SMEM((count, 2 * most), jnp.int32),
        pltpu.SMEM((count,), jnp.int32),
        *[core.AccMemorySpace(m)((cut, 2 * side), F32) for m in range(2) for _ in range(8 * cuts)],
    )


def increments(frames, basis, groups, labels, place, piece_refs, table_ref):
    for piece_ref, names in zip(piece_refs, labels):
        for n, (apart, coil_group) in enumerate(names):
            table_ref[place ^ apart, coil_group] = piece_ref[n]
    _, count, rows, lanes = table_ref.shape
    lane = lax.broadcasted_iota(jnp.int32, (count, rows, lanes), 2)

    def turned(x, by):
        return pltpu.roll(x, by % lanes, 2)

    def one(f, carry):
        sums, own = carry
        now = table_ref[f]
        behind = table_ref[jnp.maximum(f - 1, 0)]
        start = jnp.where(f == 0, turned(now, -2 * frames), turned(behind, 2 - 2 * frames))
        before = jnp.where(lane < 2, start, turned(now, 2))
        now_im, before_im = turned(now, -1), turned(before, -1)
        cross = before * now_im - before_im * now
        energy = before * before + before_im * before_im
        energy = energy + (now * now + now_im * now_im) + 1.0
        signal = 2.0 * cross / energy
        for b in range(basis):
            at = 2 * frames + 2 + b
            part = jnp.sum(now[:, :, at : at + 1] * signal, axis=0)
            part = jnp.sum(part, axis=0, keepdims=True)
            sums = sums[:b] + [jnp.where(f < place, sums[b] + part, sums[b])] + sums[b + 1 :]
            own = own[:b] + [jnp.where(f == place, part, own[b])] + own[b + 1 :]
        return sums, own

    zero = [jnp.zeros((1, lanes), F32)] * basis
    return lax.fori_loop(0, groups, one, (zero, zero), unroll=groups <= 8)


def modulate(readout, groups, labels, place_ref, owner_ref, bounds_ref, init_ref, parts_ref, *refs):
    piece_refs, refs = refs[: len(labels)], refs[len(labels) :]
    coef_ref, *out_refs, image_ref, table_ref = refs
    frames, segs, _, side, _ = parts_ref.shape
    basis = init_ref.shape[0]
    owners = len(out_refs)
    rows = side // owners
    half = side // 2
    me = owner_ref[0]
    edges = edges_of(bounds_ref, readout, segs)
    times = [(edges[l] + edges[l + 1] - 1).astype(F32) / (2.0 * readout) for l in range(segs)]
    sums, own = increments(frames, basis, groups, labels, place_ref[0], piece_refs, table_ref)
    running = []
    for b in range(basis):
        total = sums[b][:, :1]
        for t in range(1, frames):
            total = total + sums[b][:, 2 * t : 2 * t + 1]
        running.append(total)
    coef = []
    for t in range(frames):
        for b in range(basis):
            running[b] = running[b] + own[b][:, 2 * t : 2 * t + 1]
            value = init_ref[b] + running[b]
            coef.append(value)
            coef_ref[pl.ds(t * basis + b, 1), :] = jnp.broadcast_to(value, (1, coef_ref.shape[1]))
    lane = lax.broadcasted_iota(jnp.int32, (1, 128), 1)
    base = jnp.zeros((1, 128), F32)
    slope = jnp.zeros((1, 128), F32)
    scale = jnp.zeros((1, 128), F32)
    for t in range(frames):
        for l in range(segs):
            here = lane == t * segs + l
            base = jnp.where(here, coef[t * basis], base)
            slope = jnp.where(here, coef[t * basis + 1], slope)
            scale = jnp.where(here, times[l], scale)
    down_pos = (lax.broadcasted_iota(jnp.int32, (side, 128), 0) - half).astype(F32) / half
    down = (base + slope * down_pos) * scale
    cos_down, sin_down = jnp.cos(down), jnp.sin(down)
    across_pos = (lax.broadcasted_iota(jnp.int32, (1, side), 1) - half).astype(F32) / half
    across = jnp.concatenate(
        [coef[t * basis + 2] * across_pos * times[l] for t in range(frames) for l in range(segs)], axis=0
    )
    cos_across, sin_across = jnp.cos(across), jnp.sin(across)
    for t in range(frames):
        image_re = jnp.zeros((side, side), F32)
        image_im = jnp.zeros((side, side), F32)
        for l in range(segs):
            n = t * segs + l
            cr, sr = cos_down[:, n : n + 1], sin_down[:, n : n + 1]
            cc, sc = cos_across[n : n + 1], sin_across[n : n + 1]
            cos = cr * cc - sr * sc
            sin = sr * cc + cr * sc
            re, im = parts_ref[t, l, 0], parts_ref[t, l, 1]
            image_re += cos * re - sin * im
            image_im += sin * re + cos * im
        image_ref[0] = image_re
        image_ref[1] = image_im
        for d, out_ref in enumerate(out_refs):
            owned = pl.multiple_of(lax.rem(me + d, owners) * rows, rows)
            out_ref[t] = image_ref[:, pl.ds(owned, rows), :]


def around(block, axis, distance):
    count = lax.axis_size(axis)
    return lax.ppermute(block, axis, [(i, (i + distance) % count) for i in range(count)])


def exchanged(block, axis, distance):
    return lax.ppermute(block, axis, [(i, i ^ distance) for i in range(lax.axis_size(axis))])


def exchange_rounds(axis, first, size):
    rounds = []
    while first < size:
        rounds.append((axis, (2 * first, 3 * first, first) if 2 * first < size else (first,)))
        first *= 4
    return rounds


def local(kdata, angles, kernels, seg_bounds, sensitivity, ref_center, projection, init_coef):
    frames, coils, _, spokes, readout = kdata.shape
    side = kernels.shape[3]
    segs = seg_bounds.shape[0] + 1
    basis = projection.shape[0]
    owners = lax.axis_size("coils")
    starts, width = windows(readout, segs)
    right, left = (jnp.stack(jnp.split(jnp.asarray(table), 2, axis=1)) for table in dft_tables(side))
    kd = jnp.swapaxes(kdata, 2, 3)
    smem = pl.BlockSpec(memory_space=pltpu.SMEM)
    vmem = pl.BlockSpec(memory_space=pltpu.VMEM)
    place = lax.axis_index("frames").astype(jnp.int32)
    owner = lax.axis_index("coils").astype(jnp.int32)

    lanes = 128
    padded = (coils + 7) // 8 * 8
    share = pl.pallas_call(
        centres,
        grid=(1,),
        out_shape=jax.ShapeDtypeStruct((padded, lanes), F32),
        in_specs=[
            pl.BlockSpec((frames, coils, spokes, 2, lanes), lambda i: (0, 0, 0, 0, readout // 2 // lanes)),
            smem,
            smem,
        ],
        out_specs=pl.BlockSpec((padded, lanes), lambda i: (0, 0)),
        scratch_shapes=[pltpu.VMEM((2 * frames, padded, lanes), F32)],
        name="centres",
    )(kd, ref_center.T, projection)

    groups = lax.axis_size("frames")
    rounds = [("frames", (1,))] + exchange_rounds("coils", 1, owners) + exchange_rounds("frames", 2, groups)
    pieces, labels = [share[None]], [[(0, 0)]]
    for axis, distances in rounds:
        held = jnp.concatenate(pieces, axis=0) if len(pieces) > 1 else pieces[0]
        names = [name for piece in labels for name in piece]
        pieces, labels = [held], [names]
        for distance in distances:
            pieces.append(exchanged(held, axis, distance))
            labels.append([(f ^ distance, c) if axis == "frames" else (f, c ^ distance) for f, c in names])

    parts = pl.pallas_call(
        functools.partial(grid_frames, starts, width, 0, frames),
        out_shape=jax.ShapeDtypeStruct((frames, segs, 2, side, side), F32),
        in_specs=[smem, smem, vmem, vmem, vmem, vmem, vmem],
        out_specs=vmem,
        name="gridding",
    )(angles, seg_bounds, kd, kernels, right, left, sensitivity)

    block = jax.ShapeDtypeStruct((frames, 2, side // owners, side), F32)
    height = (frames * basis + 7) // 8 * 8
    coef, *blocks = pl.pallas_call(
        functools.partial(modulate, readout, groups, labels),
        out_shape=(jax.ShapeDtypeStruct((height, lanes), F32),) + (block,) * owners,
        in_specs=[smem, smem, smem, smem, vmem] + [vmem] * len(pieces),
        out_specs=(vmem,) * (1 + owners),
        scratch_shapes=[pltpu.VMEM((2, side, side), F32), pltpu.VMEM((groups, owners, padded, lanes), F32)],
        name="modulate",
    )(place.reshape(1), owner.reshape(1), seg_bounds, init_coef, parts, *pieces)
    image = blocks[0]
    for d in range(1, owners):
        image = image + around(blocks[d], "coils", d)
    field_coef = coef[: frames * basis, 0].reshape(frames, basis)
    return (image, field_coef)


def solution(mesh):
    placed = (
        P("frames", "coils", None, None, None),
        P("frames", None),
        P(),
        P(),
        P("coils", None, None, None),
        P("coils", None),
        P(None, "coils"),
        P(),
    )
    def located(*arguments):
        with jax.sharding.use_abstract_mesh(mesh.abstract_mesh):
            return local(*arguments)

    return jax.shard_map(
        local,
        mesh=mesh,
        in_specs=placed,
        out_specs=(P("frames", None, "coils", None), P("frames", None)),
        check_vma=False,
    )
```

```python
import functools
from jax._src.pallas.mosaic import core
import math

import jax
import jax.numpy as jnp
import ml_dtypes
import numpy as np
from jax import lax
from jax.experimental import pallas as pl
from jax.experimental.pallas import tpu as pltpu
from jax.sharding import PartitionSpec as P

BF16 = jnp.bfloat16
F32 = jnp.float32


def dft_tables(side):
    offsets = np.arange(side) - side // 2
    wrapped = np.mod(offsets[:, None] * offsets[None, :], side).astype(np.float32)
    phase = np.float32(2.0 * math.pi / side) * wrapped
    cosine = (np.cos(phase) / np.float32(side)).astype(ml_dtypes.bfloat16)
    sine = (np.sin(phase) / np.float32(side)).astype(ml_dtypes.bfloat16)
    right = np.block([[cosine, sine], [-sine, cosine]])
    left = np.block([[cosine, -sine], [sine, cosine]])
    return right, left


def windows(readout, segs):
    spacing, jitter = readout // segs, readout // (4 * segs)
    low = [0] + [j * spacing - jitter for j in range(1, segs)]
    high = [j * spacing + jitter for j in range(1, segs)] + [readout]
    width = 128
    while True:
        starts = [max(0, min(a // 16 * 16, readout - width)) for a in low]
        if all(s + width >= b for s, b in zip(starts, high)) or width >= readout:
            return starts, min(width, readout)
        width += 128


def edges_of(bounds_ref, readout, segs):
    return [0] + [bounds_ref[j] for j in range(segs - 1)] + [readout]


def centres(kdata_ref, first_ref, projection_ref, block_ref, center_ref):
    frames, coils = kdata_ref.shape[:2]
    rows, lanes = block_ref.shape
    basis = projection_ref.shape[0]
    lane = lax.broadcasted_iota(jnp.int32, (rows, lanes), 1)
    row = lax.broadcasted_iota(jnp.int32, (rows, lanes), 0)
    if rows > coils:
        center_ref[...] = jnp.zeros(center_ref.shape, F32)
    for t in range(frames):
        for c in range(coils):
            total = kdata_ref[t, c, 0].astype(F32)
            for s in range(1, kdata_ref.shape[2]):
                total += kdata_ref[t, c, s].astype(F32)
            for p in range(2):
                center_ref[2 * t + p, c, :] = total[p]
    block = jnp.zeros((rows, lanes), F32)
    for c in range(coils):
        values = [first_ref[p, c] for p in range(2)] + [projection_ref[b, c] for b in range(basis)]
        for n, value in enumerate(values):
            block = jnp.where((row == c) & (lane == 2 * frames + n), value, block)
    for n in range(2 * frames):
        block = jnp.where(lane == n, jnp.broadcast_to(center_ref[n][:, :1], (rows, lanes)), block)
    block_ref[...] = block


def grid_frames(starts, width, first, count, angles_ref, bounds_ref, *refs):
    *far_refs, out_ref = refs[:6]
    near_refs, sems = refs[6:11], refs[11]
    copies = [pltpu.make_async_copy(far, near, sems.at[n]) for n, (far, near) in enumerate(zip(far_refs, near_refs))]
    for copy in copies:
        copy.start()
    kdata_ref, tables_ref, right_ref, left_ref, sens_ref = near_refs
    _, coils, spokes, _, readout = kdata_ref.shape
    _, table, _, side = tables_ref.shape
    segs = len(starts)
    most = (spokes + 1) // 2
    least = min(3, most)
    pairs = coils // 2
    steps = count * pairs
    lanes = 128
    room = max(8, 2 * coils)
    group = lanes // room
    groups = (2 * most + group - 1) // group
    cut = 32
    cuts = side // cut

    def body(kd, flipped, columns, rows, weighted, halves, ky, right, left, slot_of, angle_of, tiles_of, *accs):
        banks = [[accs[(m * 8 + b) * cuts : (m * 8 + b + 1) * cuts] for b in range(8)] for m in range(2)]
        grid_acc = [banks[m][:3] for m in range(2)]
        half_acc = [banks[m][3:5] for m in range(2)]
        image_acc = [banks[m][5:] for m in range(2)]

        def multiply(bank, lhs, staged):
            for r in range(cuts):
                pltpu.matmul_acc_lhs(bank[r], lhs[r * cut : (r + 1) * cut], load_staged_rhs=None if r else staged)
        edges = edges_of(bounds_ref, readout, segs)
        index = lax.broadcasted_iota(jnp.int32, (width, side), 0)
        keep = []
        for l in range(segs):
            at = index + starts[l]
            keep.append(jnp.where((at >= edges[l]) & (at < edges[l + 1]), 1.0, 0.0).astype(BF16))

        def angle_tables(a, carry):
            ky[a] = tables_ref[1, a]
            for l in range(segs):
                rows[a, l] = (tables_ref[0, a, starts[l] : starts[l] + width, :] * keep[l]).T
            return carry

        ky[table] = jnp.zeros((readout, side), BF16)
        rows[table] = jnp.zeros((segs, side, width), BF16)
        halves[...] = jnp.zeros(halves.shape, BF16)
        out_ref[...] = jnp.zeros(out_ref.shape, F32)

        def gather(i, carry):
            kd[...] = jnp.zeros(kd.shape, F32)
            for a in range(table):
                slot_of[a] = -1
            for n in range(2 * most):
                angle_of[i, n] = table
            used = jnp.int32(0)
            for s in range(spokes):
                a = angles_ref[first + i, s]
                old = slot_of[a]
                slot = jnp.where(old < 0, used, old)
                used = used + jnp.where(old < 0, 1, 0)
                slot_of[a] = slot
                angle_of[i, slot] = a
                for c in range(coils):
                    kd[slot, 2 * c : 2 * c + 2, :] += kdata_ref[first + i, c, s].astype(F32)
            tiles_of[i] = jnp.maximum(lax.div(used + 1, 2), least)
            for g in range(groups):
                flipped[i, g] = kd[g * group : (g + 1) * group].reshape(lanes, readout).T
            return carry

        copies[0].wait()
        lax.fori_loop(0, count, gather, 0)
        copies[1].wait()
        lax.fori_loop(0, table, angle_tables, 0)
        for copy in copies[2:]:
            copy.wait()
        right[...] = right_ref[...]
        left[...] = left_ref[...]

        def place(step):
            return lax.div(step, pairs), lax.rem(step, pairs)

        def own_columns(step):
            i, n = place(step)
            for g in range(groups):
                columns[g] = pltpu.roll(flipped[i, g], lanes - 4 * n, 1).astype(BF16)

        def weigh(step, k, buf):
            i, _ = place(step)
            for e in range(2):
                slot = 2 * k + e
                factor = ky[angle_of[i, slot]]
                for m in range(2):
                    for p in range(2):
                        lane = slot % group * room + 2 * m + p
                        column = columns[slot // group, :, lane : lane + 1]
                        weighted[buf, m, p, e] = jnp.broadcast_to(column, (readout, side)) * factor

        def beside(blocks):
            return jnp.concatenate(blocks, axis=1)

        def grid_tile(step, buf, l, k):
            i, _ = place(step)
            for m in range(2):
                rhs = beside([
                    weighted[buf, m, p, :, starts[l] : starts[l] + width, :].reshape(2 * width, side) for p in range(2)
                ])
                pltpu.matmul_push_rhs(rhs, l % 2, m)
            lhs = beside([rows[angle_of[i, 2 * k + e], l] for e in range(2)])
            for m in range(2):
                multiply(grid_acc[m][l], lhs, l % 2)

        def over_columns(l):
            for m in range(2):
                pltpu.matmul_push_rhs(beside([right[0], right[1]]), 1, m)
            for r in range(cuts):
                for m in range(2):
                    gridded = pltpu.matmul_pop(grid_acc[m][l][r]).astype(BF16)
                    pltpu.matmul_acc_lhs(half_acc[m][l % 2][r], gridded, load_staged_rhs=None if r else 1)

        def keep_half(l):
            for r in range(cuts):
                for m in range(2):
                    half = pltpu.matmul_pop(half_acc[m][l % 2][r]).astype(BF16)
                    halves[m, l, 0, r * cut : (r + 1) * cut] = half[:, :side]
                    halves[m, l, 1, r * cut : (r + 1) * cut] = half[:, side:]

        def left_rows(h):
            return beside([left[q, h * side : (h + 1) * side] for q in range(2)])

        def over_rows():
            for m in range(2):
                both = beside([halves[m, l].reshape(2 * side, side) for l in range(2)])
                pltpu.matmul_push_rhs(both, 0, m)
            last = beside([halves[m, 2].reshape(2 * side, side) for m in range(2)])
            for m in range(2):
                pltpu.matmul_push_rhs(last, 1, m)
            for h in range(2):
                for m in range(2):
                    multiply(image_acc[m][h], left_rows(h), 0 if h == 0 else None)
            for m in range(2):
                multiply(image_acc[m][2], left_rows(m), 1)

        def combine(step, r):
            i, n = place(step)
            here = pl.ds(r * cut, cut)
            real = [sens_ref[2 * n + m, 0, here].astype(F32) for m in range(2)]
            imag = [sens_ref[2 * n + m, 1, here].astype(F32) for m in range(2)]

            def add(l, parts):
                total_re, total_im = out_ref[i, l, 0, here], out_ref[i, l, 1, here]
                for m in range(2):
                    re, im = parts[m]
                    total_re += real[m] * re + imag[m] * im
                    total_im += real[m] * im - imag[m] * re
                out_ref[i, l, 0, here] = total_re
                out_ref[i, l, 1, here] = total_im

            images = [[pltpu.matmul_pop(image_acc[m][h][r]) for h in range(2)] for m in range(2)]
            for l in range(2):
                add(l, [[part[:, l * side : (l + 1) * side] for part in images[m]] for m in range(2)])
            images = [pltpu.matmul_pop(image_acc[h][2][r]) for h in range(2)]
            add(2, [[part[:, m * side : (m + 1) * side] for part in images] for m in range(2)])

        def phase(tiles, step):
            earlier = jnp.maximum(step - 1, 0)
            following = jnp.minimum(step + 1, steps - 1)
            left_over = list(range(cuts))
            for k in range(tiles):
                buf = k % 2 if k else 2
                last = k == tiles - 1
                if last:
                    weigh(following, 0, 2)
                else:
                    weigh(step, k + 1, (k + 1) % 2)
                for l in range(segs):
                    grid_tile(step, buf, l, k)
                    if k == 0 and l < 2:
                        over_columns(l + 1)
                    if k >= 2 and (l or k > 2) and left_over:
                        combine(earlier, left_over.pop(0))
                    if k == tiles - 2 and l == 1:
                        own_columns(following)
                    if last and l == 1:
                        over_columns(0)
                if k == 0:
                    keep_half(1)
                    keep_half(2)
                if k == 1:
                    over_rows()
            keep_half(0)
            for r in left_over:
                combine(earlier, r)

        own_columns(0)
        weigh(0, 0, 2)

        def one(step, carry):
            i, _ = place(step)
            tiles = tiles_of[i]
            for option in range(least, most + 1):
                pl.when(tiles == option)(functools.partial(phase, option, step))
            return carry

        lax.fori_loop(0, steps, one, 0)
        over_columns(1)
        over_columns(2)
        keep_half(1)
        keep_half(2)
        over_rows()
        for r in range(cuts):
            combine(steps - 1, r)

    pl.run_scoped(
        body,
        pltpu.VMEM((groups * group, room, readout), F32),
        pltpu.VMEM((count, groups, readout, lanes), F32),
        pltpu.VMEM((groups, readout, lanes), BF16),
        pltpu.VMEM((table + 1, segs, side, width), BF16),
        pltpu.VMEM((3, 2, 2, 2, readout, side), BF16),
        pltpu.VMEM((2, segs, 2, side, side), BF16),
        pltpu.VMEM((table + 1, readout, side), BF16),
        pltpu.VMEM((2, 2 * side, side), BF16),
        pltpu.VMEM((2, 2 * side, side), BF16),
        pltpu.SMEM((table,), jnp.int32),
        pltpu.SMEM((count, 2 * most), jnp.int32),
        pltpu.SMEM((count,), jnp.int32),
        *[core.AccMemorySpace(m)((cut, 2 * side), F32) for m in range(2) for _ in range(8 * cuts)],
    )


def increments(frames, basis, groups, labels, place, piece_refs, table_ref):
    for piece_ref, names in zip(piece_refs, labels):
        for n, (apart, coil_group) in enumerate(names):
            table_ref[place ^ apart, coil_group] = piece_ref[n]
    _, count, rows, lanes = table_ref.shape
    lane = lax.broadcasted_iota(jnp.int32, (count, rows, lanes), 2)

    def turned(x, by):
        return pltpu.roll(x, by % lanes, 2)

    def one(f, carry):
        sums, own = carry
        now = table_ref[f]
        behind = table_ref[jnp.maximum(f - 1, 0)]
        start = jnp.where(f == 0, turned(now, -2 * frames), turned(behind, 2 - 2 * frames))
        before = jnp.where(lane < 2, start, turned(now, 2))
        now_im, before_im = turned(now, -1), turned(before, -1)
        cross = before * now_im - before_im * now
        energy = before * before + before_im * before_im
        energy = energy + (now * now + now_im * now_im) + 1.0
        signal = 2.0 * cross / energy
        for b in range(basis):
            at = 2 * frames + 2 + b
            part = jnp.sum(now[:, :, at : at + 1] * signal, axis=0)
            part = jnp.sum(part, axis=0, keepdims=True)
            sums = sums[:b] + [jnp.where(f < place, sums[b] + part, sums[b])] + sums[b + 1 :]
            own = own[:b] + [jnp.where(f == place, part, own[b])] + own[b + 1 :]
        return sums, own

    zero = [jnp.zeros((1, lanes), F32)] * basis
    return lax.fori_loop(0, groups, one, (zero, zero), unroll=groups <= 8)


def modulate(readout, groups, labels, place_ref, owner_ref, bounds_ref, init_ref, parts_ref, *refs):
    piece_refs, refs = refs[: len(labels)], refs[len(labels) :]
    coef_ref, *out_refs, image_ref, table_ref = refs
    frames, segs, _, side, _ = parts_ref.shape
    basis = init_ref.shape[0]
    owners = len(out_refs)
    rows = side // owners
    half = side // 2
    me = owner_ref[0]
    edges = edges_of(bounds_ref, readout, segs)
    times = [(edges[l] + edges[l + 1] - 1).astype(F32) / (2.0 * readout) for l in range(segs)]
    sums, own = increments(frames, basis, groups, labels, place_ref[0], piece_refs, table_ref)
    running = []
    for b in range(basis):
        total = sums[b][:, :1]
        for t in range(1, frames):
            total = total + sums[b][:, 2 * t : 2 * t + 1]
        running.append(total)
    coef = []
    for t in range(frames):
        for b in range(basis):
            running[b] = running[b] + own[b][:, 2 * t : 2 * t + 1]
            value = init_ref[b] + running[b]
            coef.append(value)
            coef_ref[pl.ds(t * basis + b, 1), :] = jnp.broadcast_to(value, (1, coef_ref.shape[1]))
    lane = lax.broadcasted_iota(jnp.int32, (1, 128), 1)
    base = jnp.zeros((1, 128), F32)
    slope = jnp.zeros((1, 128), F32)
    scale = jnp.zeros((1, 128), F32)
    for t in range(frames):
        for l in range(segs):
            here = lane == t * segs + l
            base = jnp.where(here, coef[t * basis], base)
            slope = jnp.where(here, coef[t * basis + 1], slope)
            scale = jnp.where(here, times[l], scale)
    down_pos = (lax.broadcasted_iota(jnp.int32, (side, 128), 0) - half).astype(F32) / half
    down = (base + slope * down_pos) * scale
    cos_down, sin_down = jnp.cos(down), jnp.sin(down)
    across_pos = (lax.broadcasted_iota(jnp.int32, (1, side), 1) - half).astype(F32) / half
    across = jnp.concatenate(
        [coef[t * basis + 2] * across_pos * times[l] for t in range(frames) for l in range(segs)], axis=0
    )
    cos_across, sin_across = jnp.cos(across), jnp.sin(across)
    for t in range(frames):
        image_re = jnp.zeros((side, side), F32)
        image_im = jnp.zeros((side, side), F32)
        for l in range(segs):
            n = t * segs + l
            cr, sr = cos_down[:, n : n + 1], sin_down[:, n : n + 1]
            cc, sc = cos_across[n : n + 1], sin_across[n : n + 1]
            cos = cr * cc - sr * sc
            sin = sr * cc + cr * sc
            re, im = parts_ref[t, l, 0], parts_ref[t, l, 1]
            image_re += cos * re - sin * im
            image_im += sin * re + cos * im
        image_ref[0] = image_re
        image_ref[1] = image_im
        for d, out_ref in enumerate(out_refs):
            owned = pl.multiple_of(lax.rem(me + d, owners) * rows, rows)
            out_ref[t] = image_ref[:, pl.ds(owned, rows), :]


def around(block, axis, distance):
    count = lax.axis_size(axis)
    return lax.ppermute(block, axis, [(i, (i + distance) % count) for i in range(count)])


def exchanged(block, axis, distance):
    return lax.ppermute(block, axis, [(i, i ^ distance) for i in range(lax.axis_size(axis))])


def exchange_rounds(axis, first, size):
    rounds = []
    while first < size:
        rounds.append((axis, (2 * first, 3 * first, first) if 2 * first < size else (first,)))
        first *= 4
    return rounds


def local(kdata, angles, kernels, seg_bounds, sensitivity, ref_center, projection, init_coef):
    frames, coils, _, spokes, readout = kdata.shape
    side = kernels.shape[3]
    segs = seg_bounds.shape[0] + 1
    basis = projection.shape[0]
    owners = lax.axis_size("coils")
    starts, width = windows(readout, segs)
    right, left = (jnp.stack(jnp.split(jnp.asarray(table), 2, axis=1)) for table in dft_tables(side))
    kd = jnp.swapaxes(kdata, 2, 3)
    smem = pl.BlockSpec(memory_space=pltpu.SMEM)
    vmem = pl.BlockSpec(memory_space=pltpu.VMEM)
    place = lax.axis_index("frames").astype(jnp.int32)
    owner = lax.axis_index("coils").astype(jnp.int32)

    lanes = 128
    padded = (coils + 7) // 8 * 8
    share = pl.pallas_call(
        centres,
        grid=(1,),
        out_shape=jax.ShapeDtypeStruct((padded, lanes), F32),
        in_specs=[
            pl.BlockSpec((frames, coils, spokes, 2, lanes), lambda i: (0, 0, 0, 0, readout // 2 // lanes)),
            smem,
            smem,
        ],
        out_specs=pl.BlockSpec((padded, lanes), lambda i: (0, 0)),
        scratch_shapes=[pltpu.VMEM((2 * frames, padded, lanes), F32)],
        name="centres",
    )(kd, ref_center.T, projection)

    groups = lax.axis_size("frames")
    rounds = [("frames", (1,))] + exchange_rounds("frames", 2, groups) + exchange_rounds("coils", 1, owners)
    pieces, labels = [share[None]], [[(0, 0)]]
    for axis, distances in rounds:
        held = jnp.concatenate(pieces, axis=0) if len(pieces) > 1 else pieces[0]
        names = [name for piece in labels for name in piece]
        pieces, labels = [held], [names]
        for distance in distances:
            pieces.append(exchanged(held, axis, distance))
            labels.append([(f ^ distance, c) if axis == "frames" else (f, c ^ distance) for f, c in names])

    parts = pl.pallas_call(
        functools.partial(grid_frames, starts, width, 0, frames),
        out_shape=jax.ShapeDtypeStruct((frames, segs, 2, side, side), F32),
        in_specs=[smem, smem] + [pl.BlockSpec(memory_space=pl.ANY)] * 5,
        out_specs=vmem,
        scratch_shapes=[pltpu.VMEM(a.shape, a.dtype) for a in (kd, kernels, right, left, sensitivity)]
        + [pltpu.SemaphoreType.DMA((5,))],
        name="gridding",
    )(angles, seg_bounds, kd, kernels, right, left, sensitivity)

    block = jax.ShapeDtypeStruct((frames, 2, side // owners, side), F32)
    height = (frames * basis + 7) // 8 * 8
    coef, *blocks = pl.pallas_call(
        functools.partial(modulate, readout, groups, labels),
        out_shape=(jax.ShapeDtypeStruct((height, lanes), F32),) + (block,) * owners,
        in_specs=[smem, smem, smem, smem, vmem] + [vmem] * len(pieces),
        out_specs=(vmem,) * (1 + owners),
        scratch_shapes=[pltpu.VMEM((2, side, side), F32), pltpu.VMEM((groups, owners, padded, lanes), F32)],
        name="modulate",
    )(place.reshape(1), owner.reshape(1), seg_bounds, init_coef, parts, *pieces)
    image = blocks[0]
    for d in range(1, owners):
        image = image + around(blocks[d], "coils", d)
    field_coef = coef[: frames * basis, 0].reshape(frames, basis)
    return (image, field_coef)


def solution(mesh):
    placed = (
        P("frames", "coils", None, None, None),
        P("frames", None),
        P(),
        P(),
        P("coils", None, None, None),
        P("coils", None),
        P(None, "coils"),
        P(),
    )
    def located(*arguments):
        with jax.sharding.use_abstract_mesh(mesh.abstract_mesh):
            return local(*arguments)

    return jax.shard_map(
        local,
        mesh=mesh,
        in_specs=placed,
        out_specs=(P("frames", None, "coils", None), P("frames", None)),
        check_vma=False,
    )
```

```python
import functools
from jax._src.pallas.mosaic import core
import math

import jax
import jax.numpy as jnp
import ml_dtypes
import numpy as np
from jax import lax
from jax.experimental import pallas as pl
from jax.experimental.pallas import tpu as pltpu
from jax.sharding import PartitionSpec as P

BF16 = jnp.bfloat16
F32 = jnp.float32


def dft_tables(side):
    offsets = np.arange(side) - side // 2
    wrapped = np.mod(offsets[:, None] * offsets[None, :], side).astype(np.float32)
    phase = np.float32(2.0 * math.pi / side) * wrapped
    cosine = (np.cos(phase) / np.float32(side)).astype(ml_dtypes.bfloat16)
    sine = (np.sin(phase) / np.float32(side)).astype(ml_dtypes.bfloat16)
    right = np.block([[cosine, sine], [-sine, cosine]])
    left = np.block([[cosine, -sine], [sine, cosine]])
    return right, left


def windows(readout, segs):
    spacing, jitter = readout // segs, readout // (4 * segs)
    low = [0] + [j * spacing - jitter for j in range(1, segs)]
    high = [j * spacing + jitter for j in range(1, segs)] + [readout]
    width = 128
    while True:
        starts = [max(0, min(a // 16 * 16, readout - width)) for a in low]
        if all(s + width >= b for s, b in zip(starts, high)) or width >= readout:
            return starts, min(width, readout)
        width += 128


def edges_of(bounds_ref, readout, segs):
    return [0] + [bounds_ref[j] for j in range(segs - 1)] + [readout]


def centres(kdata_ref, first_ref, projection_ref, block_ref, center_ref):
    frames, coils = kdata_ref.shape[:2]
    rows, lanes = block_ref.shape
    basis = projection_ref.shape[0]
    lane = lax.broadcasted_iota(jnp.int32, (rows, lanes), 1)
    row = lax.broadcasted_iota(jnp.int32, (rows, lanes), 0)
    if rows > coils:
        center_ref[...] = jnp.zeros(center_ref.shape, F32)
    for t in range(frames):
        for c in range(coils):
            total = kdata_ref[t, c, 0].astype(F32)
            for s in range(1, kdata_ref.shape[2]):
                total += kdata_ref[t, c, s].astype(F32)
            for p in range(2):
                center_ref[2 * t + p, c, :] = total[p]
    block = jnp.zeros((rows, lanes), F32)
    for c in range(coils):
        values = [first_ref[p, c] for p in range(2)] + [projection_ref[b, c] for b in range(basis)]
        for n, value in enumerate(values):
            block = jnp.where((row == c) & (lane == 2 * frames + n), value, block)
    for n in range(2 * frames):
        block = jnp.where(lane == n, jnp.broadcast_to(center_ref[n][:, :1], (rows, lanes)), block)
    block_ref[...] = block


def grid_frames(starts, width, first, count, angles_ref, bounds_ref, *refs):
    far_refs, image_ref = refs[:5], refs[5]
    near_refs, out_ref, sems, out_sems = refs[6:11], refs[11], refs[12], refs[13]
    copies = []
    for far, near in zip(far_refs, near_refs):
        parts = [(far.at[n], near.at[n]) for n in range(far.shape[0])] if len(far.shape) > 3 else [(far, near)]
        if len(far.shape) == 4 and far.shape[0] == 2:
            cut = far.shape[1] // 4
            parts = [(far.at[n, pl.ds(q * cut, cut)], near.at[n, pl.ds(q * cut, cut)]) for n in range(2) for q in range(4)]
        elif len(far.shape) == 4:
            parts = [(far, near)]
        copies.append([pltpu.make_async_copy(a, b, sems.at[len(copies), n]) for n, (a, b) in enumerate(parts)])
    for group in copies:
        for copy in group:
            copy.start()

    def arrive(n):
        for copy in copies[n]:
            copy.wait()

    kdata_ref, tables_ref, right_ref, left_ref, sens_ref = near_refs
    _, coils, spokes, _, readout = kdata_ref.shape
    _, table, _, side = tables_ref.shape
    segs = len(starts)
    most = (spokes + 1) // 2
    least = min(3, most)
    pairs = coils // 2
    steps = count * pairs
    lanes = 128
    room = max(8, 2 * coils)
    group = lanes // room
    groups = (2 * most + group - 1) // group
    cut = 16
    cuts = side // cut

    def body(sens, kd, flipped, columns, rows, weighted, halves, ky, right, left, slot_of, angle_of, tiles_of, *accs):
        banks = [[accs[(m * 8 + b) * cuts : (m * 8 + b + 1) * cuts] for b in range(8)] for m in range(2)]
        grid_acc = [banks[m][:3] for m in range(2)]
        half_acc = [banks[m][3:5] for m in range(2)]
        image_acc = [banks[m][5:] for m in range(2)]

        def multiply(bank, lhs, staged):
            for r in range(cuts):
                pltpu.matmul_acc_lhs(bank[r], lhs[r * cut : (r + 1) * cut], load_staged_rhs=None if r else staged)
        edges = edges_of(bounds_ref, readout, segs)
        index = lax.broadcasted_iota(jnp.int32, (width, side), 0)
        keep = []
        for l in range(segs):
            at = index + starts[l]
            keep.append(jnp.where((at >= edges[l]) & (at < edges[l + 1]), 1.0, 0.0).astype(BF16))

        def angle_tables(a, carry):
            ky[a] = tables_ref[1, a]
            for l in range(segs):
                rows[a, l] = (tables_ref[0, a, starts[l] : starts[l] + width, :] * keep[l]).T
            return carry

        ky[table] = jnp.zeros((readout, side), BF16)
        rows[table] = jnp.zeros((segs, side, width), BF16)
        halves[...] = jnp.zeros(halves.shape, BF16)
        out_ref[...] = jnp.zeros(out_ref.shape, F32)

        def gather(i, carry):
            kd[...] = jnp.zeros(kd.shape, F32)
            for a in range(table):
                slot_of[a] = -1
            for n in range(2 * most):
                angle_of[i, n] = table
            used = jnp.int32(0)
            for s in range(spokes):
                a = angles_ref[first + i, s]
                old = slot_of[a]
                slot = jnp.where(old < 0, used, old)
                used = used + jnp.where(old < 0, 1, 0)
                slot_of[a] = slot
                angle_of[i, slot] = a
                for c in range(coils):
                    kd[slot, 2 * c : 2 * c + 2, :] += kdata_ref[first + i, c, s].astype(F32)
            tiles_of[i] = jnp.maximum(lax.div(used + 1, 2), least)
            for g in range(groups):
                flipped[i, g] = kd[g * group : (g + 1) * group].reshape(lanes, readout).T
            return carry

        arrive(0)
        lax.fori_loop(0, count, gather, 0)
        arrive(1)
        lax.fori_loop(0, table, angle_tables, 0)
        for n in range(2, 5):
            arrive(n)
        right[...] = right_ref[...]
        left[...] = left_ref[...]
        sens[...] = sens_ref[...].astype(F32)

        def place(step):
            return lax.div(step, pairs), lax.rem(step, pairs)

        def own_columns(step):
            i, n = place(step)
            for g in range(groups):
                columns[g] = pltpu.roll(flipped[i, g], lanes - 4 * n, 1).astype(BF16)

        def weigh(step, k, buf):
            i, _ = place(step)
            for e in range(2):
                slot = 2 * k + e
                factor = ky[angle_of[i, slot]]
                for m in range(2):
                    for p in range(2):
                        lane = slot % group * room + 2 * m + p
                        column = columns[slot // group, :, lane : lane + 1]
                        weighted[buf, m, p, e] = jnp.broadcast_to(column, (readout, side)) * factor

        def beside(blocks):
            return jnp.concatenate(blocks, axis=1)

        def grid_tile(step, buf, l, k):
            i, _ = place(step)
            for m in range(2):
                rhs = beside([
                    weighted[buf, m, p, :, starts[l] : starts[l] + width, :].reshape(2 * width, side) for p in range(2)
                ])
                pltpu.matmul_push_rhs(rhs, l % 2, m)
            lhs = beside([rows[angle_of[i, 2 * k + e], l] for e in range(2)])
            for m in range(2):
                multiply(grid_acc[m][l], lhs, l % 2)

        def over_columns(l):
            for m in range(2):
                pltpu.matmul_push_rhs(beside([right[0], right[1]]), 1, m)
            for r in range(cuts):
                for m in range(2):
                    gridded = pltpu.matmul_pop(grid_acc[m][l][r]).astype(BF16)
                    pltpu.matmul_acc_lhs(half_acc[m][l % 2][r], gridded, load_staged_rhs=None if r else 1)

        def keep_half(l):
            for r in range(cuts):
                for m in range(2):
                    half = pltpu.matmul_pop(half_acc[m][l % 2][r]).astype(BF16)
                    halves[m, l, 0, r * cut : (r + 1) * cut] = half[:, :side]
                    halves[m, l, 1, r * cut : (r + 1) * cut] = half[:, side:]

        def left_rows(h):
            return beside([left[q, h * side : (h + 1) * side] for q in range(2)])

        def over_rows():
            for m in range(2):
                both = beside([halves[m, l].reshape(2 * side, side) for l in range(2)])
                pltpu.matmul_push_rhs(both, 0, m)
            last = beside([halves[m, 2].reshape(2 * side, side) for m in range(2)])
            for m in range(2):
                pltpu.matmul_push_rhs(last, 1, m)
            for h in range(2):
                for m in range(2):
                    multiply(image_acc[m][h], left_rows(h), 0 if h == 0 else None)
            for m in range(2):
                multiply(image_acc[m][2], left_rows(m), 1)

        def combine(step, r):
            i, n = place(step)
            here = pl.ds(r * cut, cut)
            real = [sens[2 * n + m, 0, here] for m in range(2)]
            imag = [sens[2 * n + m, 1, here] for m in range(2)]

            def add(l, parts):
                total_re, total_im = out_ref[i, l, 0, here], out_ref[i, l, 1, here]
                for m in range(2):
                    re, im = parts[m]
                    total_re += real[m] * re + imag[m] * im
                    total_im += real[m] * im - imag[m] * re
                out_ref[i, l, 0, here] = total_re
                out_ref[i, l, 1, here] = total_im

            images = [[pltpu.matmul_pop(image_acc[m][h][r]) for h in range(2)] for m in range(2)]
            for l in range(2):
                add(l, [[part[:, l * side : (l + 1) * side] for part in images[m]] for m in range(2)])
            images = [pltpu.matmul_pop(image_acc[h][2][r]) for h in range(2)]
            add(2, [[part[:, m * side : (m + 1) * side] for part in images] for m in range(2)])

        def phase(tiles, step):
            earlier = jnp.maximum(step - 1, 0)
            following = jnp.minimum(step + 1, steps - 1)
            left_over = list(range(cuts))
            spots = segs * tiles - 6

            for k in range(tiles):
                buf = k % 2 if k else 2
                last = k == tiles - 1
                if last:
                    weigh(following, 0, 2)
                else:
                    weigh(step, k + 1, (k + 1) % 2)
                for l in range(segs):
                    grid_tile(step, buf, l, k)
                    if k == 0 and l < 2:
                        over_columns(l + 1)
                    if k == 1 and l == 2:
                        over_rows()
                    at = k * segs + l - 6
                    if at >= 0:
                        for r in range(cuts * at // spots, cuts * (at + 1) // spots):
                            combine(earlier, r)
                    if k == tiles - 2 and l == 1:
                        own_columns(following)
                    if last and l == 1:
                        over_columns(0)
                if k == 0:
                    keep_half(1)
                    keep_half(2)
            keep_half(0)

        def leave(i):
            return pltpu.make_async_copy(out_ref.at[i], image_ref.at[i], out_sems.at[i])

        own_columns(0)
        weigh(0, 0, 2)

        def one(step, carry):
            i, _ = place(step)
            tiles = tiles_of[i]
            for option in range(least, most + 1):
                pl.when(tiles == option)(functools.partial(phase, option, step))

            @pl.when((lax.rem(step, pairs) == 0) & (step > 0))
            def _():
                leave(i - 1).start()

            return carry

        lax.fori_loop(0, steps, one, 0)
        over_columns(1)
        over_columns(2)
        keep_half(1)
        keep_half(2)
        over_rows()
        for r in range(cuts):
            combine(steps - 1, r)
        leave(count - 1).start()
        for i in range(count):
            leave(i).wait()

    pl.run_scoped(
        body,
        pltpu.VMEM((coils, 2, side, side), F32),
        pltpu.VMEM((groups * group, room, readout), F32),
        pltpu.VMEM((count, groups, readout, lanes), F32),
        pltpu.VMEM((groups, readout, lanes), BF16),
        pltpu.VMEM((table + 1, segs, side, width), BF16),
        pltpu.VMEM((3, 2, 2, 2, readout, side), BF16),
        pltpu.VMEM((2, segs, 2, side, side), BF16),
        pltpu.VMEM((table + 1, readout, side), BF16),
        pltpu.VMEM((2, 2 * side, side), BF16),
        pltpu.VMEM((2, 2 * side, side), BF16),
        pltpu.SMEM((table,), jnp.int32),
        pltpu.SMEM((count, 2 * most), jnp.int32),
        pltpu.SMEM((count,), jnp.int32),
        *[core.AccMemorySpace(m)((cut, 2 * side), F32) for m in range(2) for _ in range(8 * cuts)],
    )


def increments(frames, basis, groups, labels, place, piece_refs, table_ref):
    for piece_ref, names in zip(piece_refs, labels):
        for n, (apart, coil_group) in enumerate(names):
            table_ref[place ^ apart, coil_group] = piece_ref[n]
    _, count, rows, lanes = table_ref.shape
    lane = lax.broadcasted_iota(jnp.int32, (count, rows, lanes), 2)

    def turned(x, by):
        return pltpu.roll(x, by % lanes, 2)

    def one(f, carry):
        sums, own = carry
        now = table_ref[f]
        behind = table_ref[jnp.maximum(f - 1, 0)]
        start = jnp.where(f == 0, turned(now, -2 * frames), turned(behind, 2 - 2 * frames))
        before = jnp.where(lane < 2, start, turned(now, 2))
        now_im, before_im = turned(now, -1), turned(before, -1)
        cross = before * now_im - before_im * now
        energy = before * before + before_im * before_im
        energy = energy + (now * now + now_im * now_im) + 1.0
        signal = 2.0 * cross / energy
        for b in range(basis):
            at = 2 * frames + 2 + b
            part = jnp.sum(now[:, :, at : at + 1] * signal, axis=0)
            part = jnp.sum(part, axis=0, keepdims=True)
            sums = sums[:b] + [jnp.where(f < place, sums[b] + part, sums[b])] + sums[b + 1 :]
            own = own[:b] + [jnp.where(f == place, part, own[b])] + own[b + 1 :]
        return sums, own

    zero = [jnp.zeros((1, lanes), F32)] * basis
    return lax.fori_loop(0, groups, one, (zero, zero), unroll=groups <= 8)


def modulate(readout, groups, labels, place_ref, owner_ref, bounds_ref, init_ref, far_ref, *refs):
    piece_refs, refs = refs[: len(labels)], refs[len(labels) :]
    coef_ref, *out_refs, image_ref, table_ref, parts_ref, sems = refs
    copies = [pltpu.make_async_copy(far_ref.at[t], parts_ref.at[t], sems.at[t]) for t in range(far_ref.shape[0])]
    for copy in copies:
        copy.start()
    frames, segs, _, side, _ = parts_ref.shape
    basis = init_ref.shape[0]
    owners = len(out_refs)
    rows = side // owners
    half = side // 2
    me = owner_ref[0]
    edges = edges_of(bounds_ref, readout, segs)
    times = [(edges[l] + edges[l + 1] - 1).astype(F32) / (2.0 * readout) for l in range(segs)]
    sums, own = increments(frames, basis, groups, labels, place_ref[0], piece_refs, table_ref)
    running = []
    for b in range(basis):
        total = sums[b][:, :1]
        for t in range(1, frames):
            total = total + sums[b][:, 2 * t : 2 * t + 1]
        running.append(total)
    coef = []
    for t in range(frames):
        for b in range(basis):
            running[b] = running[b] + own[b][:, 2 * t : 2 * t + 1]
            value = init_ref[b] + running[b]
            coef.append(value)
            coef_ref[pl.ds(t * basis + b, 1), :] = jnp.broadcast_to(value, (1, coef_ref.shape[1]))
    lane = lax.broadcasted_iota(jnp.int32, (1, 128), 1)
    base = jnp.zeros((1, 128), F32)
    slope = jnp.zeros((1, 128), F32)
    scale = jnp.zeros((1, 128), F32)
    for t in range(frames):
        for l in range(segs):
            here = lane == t * segs + l
            base = jnp.where(here, coef[t * basis], base)
            slope = jnp.where(here, coef[t * basis + 1], slope)
            scale = jnp.where(here, times[l], scale)
    down_pos = (lax.broadcasted_iota(jnp.int32, (side, 128), 0) - half).astype(F32) / half
    down = (base + slope * down_pos) * scale
    cos_down, sin_down = jnp.cos(down), jnp.sin(down)
    across_pos = (lax.broadcasted_iota(jnp.int32, (1, side), 1) - half).astype(F32) / half
    across = jnp.concatenate(
        [coef[t * basis + 2] * across_pos * times[l] for t in range(frames) for l in range(segs)], axis=0
    )
    cos_across, sin_across = jnp.cos(across), jnp.sin(across)
    for t in range(frames):
        copies[t].wait()
        image_re = jnp.zeros((side, side), F32)
        image_im = jnp.zeros((side, side), F32)
        for l in range(segs):
            n = t * segs + l
            cr, sr = cos_down[:, n : n + 1], sin_down[:, n : n + 1]
            cc, sc = cos_across[n : n + 1], sin_across[n : n + 1]
            cos = cr * cc - sr * sc
            sin = sr * cc + cr * sc
            re, im = parts_ref[t, l, 0], parts_ref[t, l, 1]
            image_re += cos * re - sin * im
            image_im += sin * re + cos * im
        image_ref[0] = image_re
        image_ref[1] = image_im
        for d, out_ref in enumerate(out_refs):
            owned = pl.multiple_of(lax.rem(me + d, owners) * rows, rows)
            out_ref[t] = image_ref[:, pl.ds(owned, rows), :]


def around(block, axis, distance):
    count = lax.axis_size(axis)
    return lax.ppermute(block, axis, [(i, (i + distance) % count) for i in range(count)])


def exchanged(block, axis, distance):
    return lax.ppermute(block, axis, [(i, i ^ distance) for i in range(lax.axis_size(axis))])


def exchange_rounds(axis, first, size):
    rounds = []
    while first < size:
        rounds.append((axis, (2 * first, 3 * first, first) if 2 * first < size else (first,)))
        first *= 4
    return rounds


def local(kdata, angles, kernels, seg_bounds, sensitivity, ref_center, projection, init_coef):
    frames, coils, _, spokes, readout = kdata.shape
    side = kernels.shape[3]
    segs = seg_bounds.shape[0] + 1
    basis = projection.shape[0]
    owners = lax.axis_size("coils")
    starts, width = windows(readout, segs)
    right, left = (jnp.stack(jnp.split(jnp.asarray(table), 2, axis=1)) for table in dft_tables(side))
    kd = jnp.swapaxes(kdata, 2, 3)
    smem = pl.BlockSpec(memory_space=pltpu.SMEM)
    vmem = pl.BlockSpec(memory_space=pltpu.VMEM)
    place = lax.axis_index("frames").astype(jnp.int32)
    owner = lax.axis_index("coils").astype(jnp.int32)

    lanes = 128
    padded = (coils + 7) // 8 * 8
    share = pl.pallas_call(
        centres,
        grid=(1,),
        out_shape=jax.ShapeDtypeStruct((padded, lanes), F32),
        in_specs=[
            pl.BlockSpec((frames, coils, spokes, 2, lanes), lambda i: (0, 0, 0, 0, readout // 2 // lanes)),
            smem,
            smem,
        ],
        out_specs=pl.BlockSpec((padded, lanes), lambda i: (0, 0)),
        scratch_shapes=[pltpu.VMEM((2 * frames, padded, lanes), F32)],
        name="centres",
    )(kd, ref_center.T, projection)

    groups = lax.axis_size("frames")
    rounds = [("frames", (1,))] + exchange_rounds("frames", 2, groups) + exchange_rounds("coils", 1, owners)
    pieces, labels = [share[None]], [[(0, 0)]]
    for axis, distances in rounds:
        held = jnp.concatenate(pieces, axis=0) if len(pieces) > 1 else pieces[0]
        names = [name for piece in labels for name in piece]
        pieces, labels = [held], [names]
        for distance in distances:
            pieces.append(exchanged(held, axis, distance))
            labels.append([(f ^ distance, c) if axis == "frames" else (f, c ^ distance) for f, c in names])

    parts = pl.pallas_call(
        functools.partial(grid_frames, starts, width, 0, frames),
        out_shape=jax.ShapeDtypeStruct((frames, segs, 2, side, side), F32),
        in_specs=[smem, smem] + [pl.BlockSpec(memory_space=pl.ANY)] * 5,
        out_specs=pl.BlockSpec(memory_space=pl.ANY),
        scratch_shapes=[pltpu.VMEM(a.shape, a.dtype) for a in (kd, kernels, right, left, sensitivity)]
        + [pltpu.VMEM((frames, segs, 2, side, side), F32), pltpu.SemaphoreType.DMA((5, 8)), pltpu.SemaphoreType.DMA((frames,))],
        name="gridding",
    )(angles, seg_bounds, kd, kernels, right, left, sensitivity)

    block = jax.ShapeDtypeStruct((frames, 2, side // owners, side), F32)
    height = (frames * basis + 7) // 8 * 8
    coef, *blocks = pl.pallas_call(
        functools.partial(modulate, readout, groups, labels),
        out_shape=(jax.ShapeDtypeStruct((height, lanes), F32),) + (block,) * owners,
        in_specs=[smem, smem, smem, smem, pl.BlockSpec(memory_space=pl.ANY)] + [vmem] * len(pieces),
        out_specs=(vmem,) * (1 + owners),
        scratch_shapes=[
            pltpu.VMEM((2, side, side), F32),
            pltpu.VMEM((groups, owners, padded, lanes), F32),
            pltpu.VMEM(parts.shape, F32),
            pltpu.SemaphoreType.DMA((frames,)),
        ],
        compiler_params=pltpu.CompilerParams(vmem_limit_bytes=52 * 2**20),
        name="modulate",
    )(place.reshape(1), owner.reshape(1), seg_bounds, init_coef, parts, *pieces)
    image = blocks[0]
    for d in range(1, owners):
        image = image + around(blocks[d], "coils", d)
    field_coef = coef[: frames * basis, 0].reshape(frames, basis)
    return (image, field_coef)


def solution(mesh):
    placed = (
        P("frames", "coils", None, None, None),
        P("frames", None),
        P(),
        P(),
        P("coils", None, None, None),
        P("coils", None),
        P(None, "coils"),
        P(),
    )
    def located(*arguments):
        with jax.sharding.use_abstract_mesh(mesh.abstract_mesh):
            return local(*arguments)

    return jax.shard_map(
        local,
        mesh=mesh,
        in_specs=placed,
        out_specs=(P("frames", None, "coils", None), P("frames", None)),
        check_vma=False,
    )
```

```python
import functools
from jax._src.pallas.mosaic import core
import math

import jax
import jax.numpy as jnp
import ml_dtypes
import numpy as np
from jax import lax
from jax.experimental import pallas as pl
from jax.experimental.pallas import tpu as pltpu
from jax.sharding import PartitionSpec as P

BF16 = jnp.bfloat16
F32 = jnp.float32


def dft_tables(side):
    offsets = np.arange(side) - side // 2
    wrapped = np.mod(offsets[:, None] * offsets[None, :], side).astype(np.float32)
    phase = np.float32(2.0 * math.pi / side) * wrapped
    cosine = (np.cos(phase) / np.float32(side)).astype(ml_dtypes.bfloat16)
    sine = (np.sin(phase) / np.float32(side)).astype(ml_dtypes.bfloat16)
    right = np.block([[cosine, sine], [-sine, cosine]])
    left = np.block([[cosine, -sine], [sine, cosine]])
    return right, left


def windows(readout, segs):
    spacing, jitter = readout // segs, readout // (4 * segs)
    low = [0] + [j * spacing - jitter for j in range(1, segs)]
    high = [j * spacing + jitter for j in range(1, segs)] + [readout]
    width = 128
    while True:
        starts = [max(0, min(a // 16 * 16, readout - width)) for a in low]
        if all(s + width >= b for s, b in zip(starts, high)) or width >= readout:
            return starts, min(width, readout)
        width += 128


def edges_of(bounds_ref, readout, segs):
    return [0] + [bounds_ref[j] for j in range(segs - 1)] + [readout]


def centres(kdata_ref, first_ref, projection_ref, block_ref, center_ref):
    frames, coils = kdata_ref.shape[:2]
    rows, lanes = block_ref.shape
    basis = projection_ref.shape[0]
    lane = lax.broadcasted_iota(jnp.int32, (rows, lanes), 1)
    row = lax.broadcasted_iota(jnp.int32, (rows, lanes), 0)
    if rows > coils:
        center_ref[...] = jnp.zeros(center_ref.shape, F32)
    for t in range(frames):
        for c in range(coils):
            total = kdata_ref[t, c, 0].astype(F32)
            for s in range(1, kdata_ref.shape[2]):
                total += kdata_ref[t, c, s].astype(F32)
            for p in range(2):
                center_ref[2 * t + p, c, :] = total[p]
    block = jnp.zeros((rows, lanes), F32)
    for c in range(coils):
        values = [first_ref[p, c] for p in range(2)] + [projection_ref[b, c] for b in range(basis)]
        for n, value in enumerate(values):
            block = jnp.where((row == c) & (lane == 2 * frames + n), value, block)
    for n in range(2 * frames):
        block = jnp.where(lane == n, jnp.broadcast_to(center_ref[n][:, :1], (rows, lanes)), block)
    block_ref[...] = block


def grid_frames(starts, width, first, count, angles_ref, bounds_ref, *refs):
    far_refs, image_ref = refs[:5], refs[5]
    near_refs, out_ref, sems, out_sems = refs[6:11], refs[11], refs[12], refs[13]
    copies = []
    for far, near in zip(far_refs, near_refs):
        parts = [(far.at[n], near.at[n]) for n in range(far.shape[0])] if len(far.shape) > 3 else [(far, near)]
        if len(far.shape) == 4 and far.shape[0] == 2:
            cut = far.shape[1] // 4
            parts = [(far.at[n, pl.ds(q * cut, cut)], near.at[n, pl.ds(q * cut, cut)]) for n in range(2) for q in range(4)]
        elif len(far.shape) == 4:
            parts = [(far, near)]
        copies.append([pltpu.make_async_copy(a, b, sems.at[len(copies), n]) for n, (a, b) in enumerate(parts)])
    for group in copies:
        for copy in group:
            copy.start()

    def arrive(n):
        for copy in copies[n]:
            copy.wait()

    kdata_ref, tables_ref, right_ref, left_ref, sens_ref = near_refs
    _, coils, spokes, _, readout = kdata_ref.shape
    _, table, _, side = tables_ref.shape
    segs = len(starts)
    most = (spokes + 1) // 2
    least = min(4, most)
    pairs = coils // 2
    steps = count * pairs
    lanes = 128
    room = max(8, 2 * coils)
    group = lanes // room
    groups = (2 * most + group - 1) // group
    cut = 16
    cuts = side // cut

    def body(sens, kd, flipped, columns, rows, weighted, halves, ky, right, left, slot_of, angle_of, tiles_of, *accs):
        banks = [[accs[(m * 8 + b) * cuts : (m * 8 + b + 1) * cuts] for b in range(8)] for m in range(2)]
        grid_acc = [banks[m][:3] for m in range(2)]
        half_acc = [banks[m][3:5] for m in range(2)]
        image_acc = [banks[m][5:] for m in range(2)]

        def multiply(bank, lhs, staged):
            for r in range(cuts):
                pltpu.matmul_acc_lhs(bank[r], lhs[r * cut : (r + 1) * cut], load_staged_rhs=None if r else staged)
        edges = edges_of(bounds_ref, readout, segs)
        index = lax.broadcasted_iota(jnp.int32, (width, side), 0)
        keep = []
        for l in range(segs):
            at = index + starts[l]
            keep.append(jnp.where((at >= edges[l]) & (at < edges[l + 1]), 1.0, 0.0).astype(BF16))

        def angle_tables(a, carry):
            ky[a] = tables_ref[1, a]
            for l in range(segs):
                rows[a, l] = (tables_ref[0, a, starts[l] : starts[l] + width, :] * keep[l]).T
            return carry

        ky[table] = jnp.zeros((readout, side), BF16)
        rows[table] = jnp.zeros((segs, side, width), BF16)
        halves[...] = jnp.zeros(halves.shape, BF16)
        out_ref[...] = jnp.zeros(out_ref.shape, F32)

        def gather(i, carry):
            kd[...] = jnp.zeros(kd.shape, F32)
            for a in range(table):
                slot_of[a] = -1
            for n in range(2 * most):
                angle_of[i, n] = table
            used = jnp.int32(0)
            for s in range(spokes):
                a = angles_ref[first + i, s]
                old = slot_of[a]
                slot = jnp.where(old < 0, used, old)
                used = used + jnp.where(old < 0, 1, 0)
                slot_of[a] = slot
                angle_of[i, slot] = a
                for c in range(coils):
                    kd[slot, 2 * c : 2 * c + 2, :] += kdata_ref[first + i, c, s].astype(F32)
            tiles_of[i] = jnp.maximum(lax.div(used + 1, 2), least)
            for g in range(groups):
                flipped[i, g] = kd[g * group : (g + 1) * group].reshape(lanes, readout).T
            return carry

        arrive(0)
        lax.fori_loop(0, count, gather, 0)
        arrive(1)
        lax.fori_loop(0, table, angle_tables, 0)
        for n in range(2, 5):
            arrive(n)
        right[...] = right_ref[...]
        left[...] = left_ref[...]
        sens[...] = sens_ref[...].astype(F32)

        def place(step):
            return lax.div(step, pairs), lax.rem(step, pairs)

        def own_columns(step):
            i, n = place(step)
            for g in range(groups):
                columns[g] = pltpu.roll(flipped[i, g], lanes - 4 * n, 1).astype(BF16)

        def weigh(step, k, buf):
            i, _ = place(step)
            for e in range(2):
                slot = 2 * k + e
                factor = ky[angle_of[i, slot]]
                for m in range(2):
                    for p in range(2):
                        lane = slot % group * room + 2 * m + p
                        column = columns[slot // group, :, lane : lane + 1]
                        weighted[buf, m, p, e] = jnp.broadcast_to(column, (readout, side)) * factor

        def beside(blocks):
            return jnp.concatenate(blocks, axis=1)

        def grid_tile(step, buf, l, k):
            i, _ = place(step)
            for m in range(2):
                rhs = beside([
                    weighted[buf, m, p, :, starts[l] : starts[l] + width, :].reshape(2 * width, side) for p in range(2)
                ])
                pltpu.matmul_push_rhs(rhs, l % 2, m)
            lhs = beside([rows[angle_of[i, 2 * k + e], l] for e in range(2)])
            for m in range(2):
                multiply(grid_acc[m][l], lhs, l % 2)

        def over_columns(l):
            for m in range(2):
                pltpu.matmul_push_rhs(beside([right[0], right[1]]), 1, m)
            for r in range(cuts):
                for m in range(2):
                    gridded = pltpu.matmul_pop(grid_acc[m][l][r]).astype(BF16)
                    pltpu.matmul_acc_lhs(half_acc[m][l % 2][r], gridded, load_staged_rhs=None if r else 1)

        def keep_half(l):
            for r in range(cuts):
                for m in range(2):
                    half = pltpu.matmul_pop(half_acc[m][l % 2][r]).astype(BF16)
                    halves[m, l, 0, r * cut : (r + 1) * cut] = half[:, :side]
                    halves[m, l, 1, r * cut : (r + 1) * cut] = half[:, side:]

        def left_rows(h):
            return beside([left[q, h * side : (h + 1) * side] for q in range(2)])

        def over_rows():
            for m in range(2):
                both = beside([halves[m, l].reshape(2 * side, side) for l in range(2)])
                pltpu.matmul_push_rhs(both, 0, m)
            last = beside([halves[m, 2].reshape(2 * side, side) for m in range(2)])
            for m in range(2):
                pltpu.matmul_push_rhs(last, 1, m)
            for h in range(2):
                for m in range(2):
                    multiply(image_acc[m][h], left_rows(h), 0 if h == 0 else None)
            for m in range(2):
                multiply(image_acc[m][2], left_rows(m), 1)

        def combine(step, r):
            i, n = place(step)
            here = pl.ds(r * cut, cut)
            real = [sens[2 * n + m, 0, here] for m in range(2)]
            imag = [sens[2 * n + m, 1, here] for m in range(2)]

            def add(l, parts):
                total_re, total_im = out_ref[i, l, 0, here], out_ref[i, l, 1, here]
                for m in range(2):
                    re, im = parts[m]
                    total_re += real[m] * re + imag[m] * im
                    total_im += real[m] * im - imag[m] * re
                out_ref[i, l, 0, here] = total_re
                out_ref[i, l, 1, here] = total_im

            images = [[pltpu.matmul_pop(image_acc[m][h][r]) for h in range(2)] for m in range(2)]
            for l in range(2):
                add(l, [[part[:, l * side : (l + 1) * side] for part in images[m]] for m in range(2)])
            images = [pltpu.matmul_pop(image_acc[h][2][r]) for h in range(2)]
            add(2, [[part[:, m * side : (m + 1) * side] for part in images] for m in range(2)])

        def phase(tiles, step):
            earlier = jnp.maximum(step - 1, 0)
            following = jnp.minimum(step + 1, steps - 1)
            left_over = list(range(cuts))
            spots = segs * tiles - 6

            for k in range(tiles):
                buf = k % 2 if k else 2
                last = k == tiles - 1
                if last:
                    weigh(following, 0, 2)
                else:
                    weigh(step, k + 1, (k + 1) % 2)
                for l in range(segs):
                    grid_tile(step, buf, l, k)
                    if k == 0 and l < 2:
                        over_columns(l + 1)
                    if k == 1 and l == 2:
                        over_rows()
                    at = k * segs + l - 6
                    if at >= 0:
                        for r in range(cuts * at // spots, cuts * (at + 1) // spots):
                            combine(earlier, r)
                    if k == tiles - 2 and l == 1:
                        own_columns(following)
                    if last and l == 1:
                        over_columns(0)
                if k == 0:
                    keep_half(1)
                    keep_half(2)
            keep_half(0)

        def leave(i):
            return pltpu.make_async_copy(out_ref.at[i], image_ref.at[i], out_sems.at[i])

        own_columns(0)
        weigh(0, 0, 2)

        together = pairs

        def several(tiles, step):
            for n in range(together):
                phase(tiles, step + n)

        def one(q, carry):
            step = q * together
            i, n = place(step)
            tiles = tiles_of[i]
            for option in range(least, most + 1):
                pl.when(tiles == option)(functools.partial(several, option, step))

            @pl.when((n == 0) & (i > 0))
            def _():
                leave(i - 1).start()

            return carry

        lax.fori_loop(0, steps // together, one, 0)
        over_columns(1)
        over_columns(2)
        keep_half(1)
        keep_half(2)
        over_rows()
        for r in range(cuts):
            combine(steps - 1, r)
        leave(count - 1).start()
        for i in range(count):
            leave(i).wait()

    pl.run_scoped(
        body,
        pltpu.VMEM((coils, 2, side, side), F32),
        pltpu.VMEM((groups * group, room, readout), F32),
        pltpu.VMEM((count, groups, readout, lanes), F32),
        pltpu.VMEM((groups, readout, lanes), BF16),
        pltpu.VMEM((table + 1, segs, side, width), BF16),
        pltpu.VMEM((3, 2, 2, 2, readout, side), BF16),
        pltpu.VMEM((2, segs, 2, side, side), BF16),
        pltpu.VMEM((table + 1, readout, side), BF16),
        pltpu.VMEM((2, 2 * side, side), BF16),
        pltpu.VMEM((2, 2 * side, side), BF16),
        pltpu.SMEM((table,), jnp.int32),
        pltpu.SMEM((count, 2 * most), jnp.int32),
        pltpu.SMEM((count,), jnp.int32),
        *[core.AccMemorySpace(m)((cut, 2 * side), F32) for m in range(2) for _ in range(8 * cuts)],
    )


def increments(frames, basis, groups, labels, place, piece_refs, table_ref):
    for piece_ref, names in zip(piece_refs, labels):
        for n, (apart, coil_group) in enumerate(names):
            table_ref[place ^ apart, coil_group] = piece_ref[n]
    _, count, rows, lanes = table_ref.shape
    lane = lax.broadcasted_iota(jnp.int32, (count, rows, lanes), 2)

    def turned(x, by):
        return pltpu.roll(x, by % lanes, 2)

    def one(f, carry):
        sums, own = carry
        now = table_ref[f]
        behind = table_ref[jnp.maximum(f - 1, 0)]
        start = jnp.where(f == 0, turned(now, -2 * frames), turned(behind, 2 - 2 * frames))
        before = jnp.where(lane < 2, start, turned(now, 2))
        now_im, before_im = turned(now, -1), turned(before, -1)
        cross = before * now_im - before_im * now
        energy = before * before + before_im * before_im
        energy = energy + (now * now + now_im * now_im) + 1.0
        signal = 2.0 * cross / energy
        for b in range(basis):
            at = 2 * frames + 2 + b
            part = jnp.sum(now[:, :, at : at + 1] * signal, axis=0)
            part = jnp.sum(part, axis=0, keepdims=True)
            sums = sums[:b] + [jnp.where(f < place, sums[b] + part, sums[b])] + sums[b + 1 :]
            own = own[:b] + [jnp.where(f == place, part, own[b])] + own[b + 1 :]
        return sums, own

    zero = [jnp.zeros((1, lanes), F32)] * basis
    return lax.fori_loop(0, groups, one, (zero, zero), unroll=groups <= 8)


def modulate(readout, groups, labels, place_ref, owner_ref, bounds_ref, init_ref, far_ref, *refs):
    piece_refs, refs = refs[: len(labels)], refs[len(labels) :]
    coef_ref, *out_refs, image_ref, table_ref, parts_ref, sems = refs
    copies = [pltpu.make_async_copy(far_ref.at[t], parts_ref.at[t], sems.at[t]) for t in range(far_ref.shape[0])]
    for copy in copies:
        copy.start()
    frames, segs, _, side, _ = parts_ref.shape
    basis = init_ref.shape[0]
    owners = len(out_refs)
    rows = side // owners
    half = side // 2
    me = owner_ref[0]
    edges = edges_of(bounds_ref, readout, segs)
    times = [(edges[l] + edges[l + 1] - 1).astype(F32) / (2.0 * readout) for l in range(segs)]
    sums, own = increments(frames, basis, groups, labels, place_ref[0], piece_refs, table_ref)
    running = []
    for b in range(basis):
        total = sums[b][:, :1]
        for t in range(1, frames):
            total = total + sums[b][:, 2 * t : 2 * t + 1]
        running.append(total)
    coef = []
    for t in range(frames):
        for b in range(basis):
            running[b] = running[b] + own[b][:, 2 * t : 2 * t + 1]
            value = init_ref[b] + running[b]
            coef.append(value)
            coef_ref[pl.ds(t * basis + b, 1), :] = jnp.broadcast_to(value, (1, coef_ref.shape[1]))
    lane = lax.broadcasted_iota(jnp.int32, (1, 128), 1)
    base = jnp.zeros((1, 128), F32)
    slope = jnp.zeros((1, 128), F32)
    scale = jnp.zeros((1, 128), F32)
    for t in range(frames):
        for l in range(segs):
            here = lane == t * segs + l
            base = jnp.where(here, coef[t * basis], base)
            slope = jnp.where(here, coef[t * basis + 1], slope)
            scale = jnp.where(here, times[l], scale)
    down_pos = (lax.broadcasted_iota(jnp.int32, (side, 128), 0) - half).astype(F32) / half
    down = (base + slope * down_pos) * scale
    cos_down, sin_down = jnp.cos(down), jnp.sin(down)
    across_pos = (lax.broadcasted_iota(jnp.int32, (1, side), 1) - half).astype(F32) / half
    across = jnp.concatenate(
        [coef[t * basis + 2] * across_pos * times[l] for t in range(frames) for l in range(segs)], axis=0
    )
    cos_across, sin_across = jnp.cos(across), jnp.sin(across)
    for t in range(frames):
        copies[t].wait()
        image_re = jnp.zeros((side, side), F32)
        image_im = jnp.zeros((side, side), F32)
        for l in range(segs):
            n = t * segs + l
            cr, sr = cos_down[:, n : n + 1], sin_down[:, n : n + 1]
            cc, sc = cos_across[n : n + 1], sin_across[n : n + 1]
            cos = cr * cc - sr * sc
            sin = sr * cc + cr * sc
            re, im = parts_ref[t, l, 0], parts_ref[t, l, 1]
            image_re += cos * re - sin * im
            image_im += sin * re + cos * im
        image_ref[0] = image_re
        image_ref[1] = image_im
        for d, out_ref in enumerate(out_refs):
            owned = pl.multiple_of(lax.rem(me + d, owners) * rows, rows)
            out_ref[t] = image_ref[:, pl.ds(owned, rows), :]


def around(block, axis, distance):
    count = lax.axis_size(axis)
    return lax.ppermute(block, axis, [(i, (i + distance) % count) for i in range(count)])


def exchanged(block, axis, distance):
    return lax.ppermute(block, axis, [(i, i ^ distance) for i in range(lax.axis_size(axis))])


def exchange_rounds(axis, first, size):
    rounds = []
    while first < size:
        rounds.append((axis, (2 * first, 3 * first, first) if 2 * first < size else (first,)))
        first *= 4
    return rounds


def local(kdata, angles, kernels, seg_bounds, sensitivity, ref_center, projection, init_coef):
    frames, coils, _, spokes, readout = kdata.shape
    side = kernels.shape[3]
    segs = seg_bounds.shape[0] + 1
    basis = projection.shape[0]
    owners = lax.axis_size("coils")
    starts, width = windows(readout, segs)
    right, left = (jnp.stack(jnp.split(jnp.asarray(table), 2, axis=1)) for table in dft_tables(side))
    kd = jnp.swapaxes(kdata, 2, 3)
    smem = pl.BlockSpec(memory_space=pltpu.SMEM)
    vmem = pl.BlockSpec(memory_space=pltpu.VMEM)
    place = lax.axis_index("frames").astype(jnp.int32)
    owner = lax.axis_index("coils").astype(jnp.int32)

    lanes = 128
    padded = (coils + 7) // 8 * 8
    share = pl.pallas_call(
        centres,
        grid=(1,),
        out_shape=jax.ShapeDtypeStruct((padded, lanes), F32),
        in_specs=[
            pl.BlockSpec((frames, coils, spokes, 2, lanes), lambda i: (0, 0, 0, 0, readout // 2 // lanes)),
            smem,
            smem,
        ],
        out_specs=pl.BlockSpec((padded, lanes), lambda i: (0, 0)),
        scratch_shapes=[pltpu.VMEM((2 * frames, padded, lanes), F32)],
        name="centres",
    )(kd, ref_center.T, projection)

    groups = lax.axis_size("frames")
    rounds = [("frames", (1,))] + exchange_rounds("frames", 2, groups) + exchange_rounds("coils", 1, owners)
    pieces, labels = [share[None]], [[(0, 0)]]
    for axis, distances in rounds:
        held = jnp.concatenate(pieces, axis=0) if len(pieces) > 1 else pieces[0]
        names = [name for piece in labels for name in piece]
        pieces, labels = [held], [names]
        for distance in distances:
            pieces.append(exchanged(held, axis, distance))
            labels.append([(f ^ distance, c) if axis == "frames" else (f, c ^ distance) for f, c in names])

    parts = pl.pallas_call(
        functools.partial(grid_frames, starts, width, 0, frames),
        out_shape=jax.ShapeDtypeStruct((frames, segs, 2, side, side), F32),
        in_specs=[smem, smem] + [pl.BlockSpec(memory_space=pl.ANY)] * 5,
        out_specs=pl.BlockSpec(memory_space=pl.ANY),
        scratch_shapes=[pltpu.VMEM(a.shape, a.dtype) for a in (kd, kernels, right, left, sensitivity)]
        + [pltpu.VMEM((frames, segs, 2, side, side), F32), pltpu.SemaphoreType.DMA((5, 8)), pltpu.SemaphoreType.DMA((frames,))],
        name="gridding",
    )(angles, seg_bounds, kd, kernels, right, left, sensitivity)

    block = jax.ShapeDtypeStruct((frames, 2, side // owners, side), F32)
    height = (frames * basis + 7) // 8 * 8
    coef, *blocks = pl.pallas_call(
        functools.partial(modulate, readout, groups, labels),
        out_shape=(jax.ShapeDtypeStruct((height, lanes), F32),) + (block,) * owners,
        in_specs=[smem, smem, smem, smem, pl.BlockSpec(memory_space=pl.ANY)] + [vmem] * len(pieces),
        out_specs=(vmem,) * (1 + owners),
        scratch_shapes=[
            pltpu.VMEM((2, side, side), F32),
            pltpu.VMEM((groups, owners, padded, lanes), F32),
            pltpu.VMEM(parts.shape, F32),
            pltpu.SemaphoreType.DMA((frames,)),
        ],
        compiler_params=pltpu.CompilerParams(vmem_limit_bytes=52 * 2**20),
        name="modulate",
    )(place.reshape(1), owner.reshape(1), seg_bounds, init_coef, parts, *pieces)
    image = blocks[0]
    for d in range(1, owners):
        image = image + around(blocks[d], "coils", d)
    field_coef = coef[: frames * basis, 0].reshape(frames, basis)
    return (image, field_coef)


def solution(mesh):
    placed = (
        P("frames", "coils", None, None, None),
        P("frames", None),
        P(),
        P(),
        P("coils", None, None, None),
        P("coils", None),
        P(None, "coils"),
        P(),
    )
    def located(*arguments):
        with jax.sharding.use_abstract_mesh(mesh.abstract_mesh):
            return local(*arguments)

    return jax.shard_map(
        local,
        mesh=mesh,
        in_specs=placed,
        out_specs=(P("frames", None, "coils", None), P("frames", None)),
        check_vma=False,
    )
```

```python
import functools
from jax._src.pallas.mosaic import core
import math

import jax
import jax.numpy as jnp
import ml_dtypes
import numpy as np
from jax import lax
from jax.experimental import pallas as pl
from jax.experimental.pallas import tpu as pltpu
from jax.sharding import PartitionSpec as P

BF16 = jnp.bfloat16
F32 = jnp.float32


def dft_tables(side):
    offsets = np.arange(side) - side // 2
    wrapped = np.mod(offsets[:, None] * offsets[None, :], side).astype(np.float32)
    phase = np.float32(2.0 * math.pi / side) * wrapped
    cosine = (np.cos(phase) / np.float32(side)).astype(ml_dtypes.bfloat16)
    sine = (np.sin(phase) / np.float32(side)).astype(ml_dtypes.bfloat16)
    right = np.block([[cosine, sine], [-sine, cosine]])
    left = np.block([[cosine, -sine], [sine, cosine]])
    return right, left


def windows(readout, segs):
    spacing, jitter = readout // segs, readout // (4 * segs)
    low = [0] + [j * spacing - jitter for j in range(1, segs)]
    high = [j * spacing + jitter for j in range(1, segs)] + [readout]
    width = 128
    while True:
        starts = [max(0, min(a // 16 * 16, readout - width)) for a in low]
        if all(s + width >= b for s, b in zip(starts, high)) or width >= readout:
            return starts, min(width, readout)
        width += 128


def edges_of(bounds_ref, readout, segs):
    return [0] + [bounds_ref[j] for j in range(segs - 1)] + [readout]


def centres(kdata_ref, first_ref, projection_ref, block_ref, center_ref):
    frames, coils = kdata_ref.shape[:2]
    rows, lanes = block_ref.shape
    basis = projection_ref.shape[0]
    lane = lax.broadcasted_iota(jnp.int32, (rows, lanes), 1)
    row = lax.broadcasted_iota(jnp.int32, (rows, lanes), 0)
    if rows > coils:
        center_ref[...] = jnp.zeros(center_ref.shape, F32)
    for t in range(frames):
        for c in range(coils):
            total = kdata_ref[t, c, 0].astype(F32)
            for s in range(1, kdata_ref.shape[2]):
                total += kdata_ref[t, c, s].astype(F32)
            for p in range(2):
                center_ref[2 * t + p, c, :] = total[p]
    block = jnp.zeros((rows, lanes), F32)
    for c in range(coils):
        values = [first_ref[p, c] for p in range(2)] + [projection_ref[b, c] for b in range(basis)]
        for n, value in enumerate(values):
            block = jnp.where((row == c) & (lane == 2 * frames + n), value, block)
    for n in range(2 * frames):
        block = jnp.where(lane == n, jnp.broadcast_to(center_ref[n][:, :1], (rows, lanes)), block)
    block_ref[...] = block


def grid_frames(starts, width, first, count, angles_ref, bounds_ref, *refs):
    far_refs, image_ref = refs[:5], refs[5]
    near_refs, out_ref, sems, out_sems = refs[6:11], refs[11], refs[12], refs[13]
    copies = []
    for far, near in zip(far_refs, near_refs):
        parts = [(far.at[n], near.at[n]) for n in range(far.shape[0])] if len(far.shape) > 3 else [(far, near)]
        if len(far.shape) == 4 and far.shape[0] == 2:
            cut = far.shape[1] // 4
            parts = [(far.at[n, pl.ds(q * cut, cut)], near.at[n, pl.ds(q * cut, cut)]) for q in range(4) for n in range(2)]
        elif len(far.shape) == 4:
            parts = [(far, near)]
        copies.append([pltpu.make_async_copy(a, b, sems.at[len(copies), n]) for n, (a, b) in enumerate(parts)])
    for group in copies:
        for copy in group:
            copy.start()

    def arrive(n):
        for copy in copies[n]:
            copy.wait()

    kdata_ref, tables_ref, right_ref, left_ref, sens_ref = near_refs
    _, coils, spokes, _, readout = kdata_ref.shape
    _, table, _, side = tables_ref.shape
    segs = len(starts)
    most = (spokes + 1) // 2
    least = min(4, most)
    pairs = coils // 2
    steps = count * pairs
    lanes = 128
    room = max(8, 2 * coils)
    group = lanes // room
    groups = (2 * most + group - 1) // group
    cut = 16
    cuts = side // cut

    def body(sens, kd, flipped, columns, rows, weighted, halves, ky, right, left, slot_of, angle_of, tiles_of, *accs):
        banks = [[accs[(m * 8 + b) * cuts : (m * 8 + b + 1) * cuts] for b in range(8)] for m in range(2)]
        grid_acc = [banks[m][:3] for m in range(2)]
        half_acc = [banks[m][3:5] for m in range(2)]
        image_acc = [banks[m][5:] for m in range(2)]

        def multiply(bank, lhs, staged):
            for r in range(cuts):
                pltpu.matmul_acc_lhs(bank[r], lhs[r * cut : (r + 1) * cut], load_staged_rhs=None if r else staged)
        edges = edges_of(bounds_ref, readout, segs)
        index = lax.broadcasted_iota(jnp.int32, (width, side), 0)
        keep = []
        for l in range(segs):
            at = index + starts[l]
            keep.append(jnp.where((at >= edges[l]) & (at < edges[l + 1]), 1.0, 0.0).astype(BF16))

        def angle_tables(a, carry):
            ky[a] = tables_ref[1, a]
            for l in range(segs):
                rows[a, l] = (tables_ref[0, a, starts[l] : starts[l] + width, :] * keep[l]).T
            return carry

        for bank in banks[0] + banks[1]:
            for acc in bank:
                pltpu.matmul_pop(acc)
        ky[table] = jnp.zeros((readout, side), BF16)
        rows[table] = jnp.zeros((segs, side, width), BF16)
        halves[...] = jnp.zeros(halves.shape, BF16)
        out_ref[...] = jnp.zeros(out_ref.shape, F32)

        def gather(i, carry):
            kd[...] = jnp.zeros(kd.shape, F32)
            for a in range(table):
                slot_of[a] = -1
            for n in range(2 * most):
                angle_of[i, n] = table
            used = jnp.int32(0)
            for s in range(spokes):
                a = angles_ref[first + i, s]
                old = slot_of[a]
                slot = jnp.where(old < 0, used, old)
                used = used + jnp.where(old < 0, 1, 0)
                slot_of[a] = slot
                angle_of[i, slot] = a
                for c in range(coils):
                    kd[slot, 2 * c : 2 * c + 2, :] += kdata_ref[first + i, c, s].astype(F32)
            tiles_of[i] = jnp.maximum(lax.div(used + 1, 2), least)
            for g in range(groups):
                flipped[i, g] = kd[g * group : (g + 1) * group].reshape(lanes, readout).T
            return carry

        arrive(0)
        lax.fori_loop(0, count, gather, 0)
        for q in range(4):
            for copy in copies[1][2 * q : 2 * q + 2]:
                copy.wait()
            lax.fori_loop(table * q // 4, table * (q + 1) // 4, angle_tables, 0)
        for n in range(2, 5):
            arrive(n)
        right[...] = right_ref[...]
        left[...] = left_ref[...]
        sens[...] = sens_ref[...].astype(F32)

        def place(step):
            return lax.div(step, pairs), lax.rem(step, pairs)

        def own_columns(step):
            i, n = place(step)
            for g in range(groups):
                columns[g] = pltpu.roll(flipped[i, g], lanes - 4 * n, 1).astype(BF16)

        def weigh(step, k, buf):
            i, _ = place(step)
            for e in range(2):
                slot = 2 * k + e
                factor = ky[angle_of[i, slot]]
                for m in range(2):
                    for p in range(2):
                        lane = slot % group * room + 2 * m + p
                        column = columns[slot // group, :, lane : lane + 1]
                        weighted[buf, m, p, e] = jnp.broadcast_to(column, (readout, side)) * factor

        def beside(blocks):
            return jnp.concatenate(blocks, axis=1)

        def grid_tile(step, buf, l, k):
            i, _ = place(step)
            for m in range(2):
                rhs = beside([
                    weighted[buf, m, p, :, starts[l] : starts[l] + width, :].reshape(2 * width, side) for p in range(2)
                ])
                pltpu.matmul_push_rhs(rhs, l % 2, m)
            lhs = beside([rows[angle_of[i, 2 * k + e], l] for e in range(2)])
            for m in range(2):
                multiply(grid_acc[m][l], lhs, l % 2)

        def over_columns(l):
            for m in range(2):
                pltpu.matmul_push_rhs(beside([right[0], right[1]]), 1, m)
            for r in range(cuts):
                for m in range(2):
                    gridded = pltpu.matmul_pop(grid_acc[m][l][r]).astype(BF16)
                    pltpu.matmul_acc_lhs(half_acc[m][l % 2][r], gridded, load_staged_rhs=None if r else 1)

        def keep_half(l):
            for r in range(cuts):
                for m in range(2):
                    half = pltpu.matmul_pop(half_acc[m][l % 2][r]).astype(BF16)
                    halves[m, l, 0, r * cut : (r + 1) * cut] = half[:, :side]
                    halves[m, l, 1, r * cut : (r + 1) * cut] = half[:, side:]

        def left_rows(h):
            return beside([left[q, h * side : (h + 1) * side] for q in range(2)])

        def over_rows():
            for m in range(2):
                both = beside([halves[m, l].reshape(2 * side, side) for l in range(2)])
                pltpu.matmul_push_rhs(both, 0, m)
            last = beside([halves[m, 2].reshape(2 * side, side) for m in range(2)])
            for m in range(2):
                pltpu.matmul_push_rhs(last, 1, m)
            for h in range(2):
                for m in range(2):
                    multiply(image_acc[m][h], left_rows(h), 0 if h == 0 else None)
            for m in range(2):
                multiply(image_acc[m][2], left_rows(m), 1)

        def combine(step, r):
            i, n = place(step)
            here = pl.ds(r * cut, cut)
            real = [sens[2 * n + m, 0, here] for m in range(2)]
            imag = [sens[2 * n + m, 1, here] for m in range(2)]

            def add(l, parts):
                total_re, total_im = out_ref[i, l, 0, here], out_ref[i, l, 1, here]
                for m in range(2):
                    re, im = parts[m]
                    total_re += real[m] * re + imag[m] * im
                    total_im += real[m] * im - imag[m] * re
                out_ref[i, l, 0, here] = total_re
                out_ref[i, l, 1, here] = total_im

            images = [[pltpu.matmul_pop(image_acc[m][h][r]) for h in range(2)] for m in range(2)]
            for l in range(2):
                add(l, [[part[:, l * side : (l + 1) * side] for part in images[m]] for m in range(2)])
            images = [pltpu.matmul_pop(image_acc[h][2][r]) for h in range(2)]
            add(2, [[part[:, m * side : (m + 1) * side] for part in images] for m in range(2)])

        def phase(tiles, step):
            earlier = jnp.maximum(step - 1, 0)
            following = jnp.minimum(step + 1, steps - 1)
            left_over = list(range(cuts))
            spots = segs * tiles - 6

            for k in range(tiles):
                buf = k % 2 if k else 2
                last = k == tiles - 1
                if last:
                    weigh(following, 0, 2)
                else:
                    weigh(step, k + 1, (k + 1) % 2)
                for l in range(segs):
                    grid_tile(step, buf, l, k)
                    if k == 0 and l < 2:
                        over_columns(l + 1)
                    if k == 1 and l == 2:
                        over_rows()
                    at = k * segs + l - 6
                    if at >= 0:
                        for r in range(cuts * at // spots, cuts * (at + 1) // spots):
                            combine(earlier, r)
                    if k == tiles - 2 and l == 1:
                        own_columns(following)
                    if last and l == 1:
                        over_columns(0)
                if k == 0:
                    keep_half(1)
                    keep_half(2)
            keep_half(0)

        def leave(i):
            return pltpu.make_async_copy(out_ref.at[i], image_ref.at[i], out_sems.at[i])

        own_columns(0)
        weigh(0, 0, 2)

        together = pairs

        def several(tiles, step):
            for n in range(together):
                phase(tiles, step + n)

        def one(q, carry):
            step = q * together
            i, n = place(step)
            tiles = tiles_of[i]
            for option in range(least, most + 1):
                pl.when(tiles == option)(functools.partial(several, option, step))

            @pl.when((n == 0) & (i > 0))
            def _():
                leave(i - 1).start()

            return carry

        lax.fori_loop(0, steps // together, one, 0)
        over_columns(1)
        over_columns(2)
        keep_half(1)
        keep_half(2)
        over_rows()
        for r in range(cuts):
            combine(steps - 1, r)
        leave(count - 1).start()
        for i in range(count):
            leave(i).wait()

    pl.run_scoped(
        body,
        pltpu.VMEM((coils, 2, side, side), F32),
        pltpu.VMEM((groups * group, room, readout), F32),
        pltpu.VMEM((count, groups, readout, lanes), F32),
        pltpu.VMEM((groups, readout, lanes), BF16),
        pltpu.VMEM((table + 1, segs, side, width), BF16),
        pltpu.VMEM((3, 2, 2, 2, readout, side), BF16),
        pltpu.VMEM((2, segs, 2, side, side), BF16),
        pltpu.VMEM((table + 1, readout, side), BF16),
        pltpu.VMEM((2, 2 * side, side), BF16),
        pltpu.VMEM((2, 2 * side, side), BF16),
        pltpu.SMEM((table,), jnp.int32),
        pltpu.SMEM((count, 2 * most), jnp.int32),
        pltpu.SMEM((count,), jnp.int32),
        *[core.AccMemorySpace(m)((cut, 2 * side), F32) for m in range(2) for _ in range(8 * cuts)],
    )


def increments(frames, basis, groups, labels, place, piece_refs, table_ref):
    for piece_ref, names in zip(piece_refs, labels):
        for n, (apart, coil_group) in enumerate(names):
            table_ref[place ^ apart, coil_group] = piece_ref[n]
    _, count, rows, lanes = table_ref.shape
    lane = lax.broadcasted_iota(jnp.int32, (count, rows, lanes), 2)

    def turned(x, by):
        return pltpu.roll(x, by % lanes, 2)

    def one(f, carry):
        sums, own = carry
        now = table_ref[f]
        behind = table_ref[jnp.maximum(f - 1, 0)]
        start = jnp.where(f == 0, turned(now, -2 * frames), turned(behind, 2 - 2 * frames))
        before = jnp.where(lane < 2, start, turned(now, 2))
        now_im, before_im = turned(now, -1), turned(before, -1)
        cross = before * now_im - before_im * now
        energy = before * before + before_im * before_im
        energy = energy + (now * now + now_im * now_im) + 1.0
        signal = 2.0 * cross / energy
        for b in range(basis):
            at = 2 * frames + 2 + b
            part = jnp.sum(now[:, :, at : at + 1] * signal, axis=0)
            part = jnp.sum(part, axis=0, keepdims=True)
            sums = sums[:b] + [jnp.where(f < place, sums[b] + part, sums[b])] + sums[b + 1 :]
            own = own[:b] + [jnp.where(f == place, part, own[b])] + own[b + 1 :]
        return sums, own

    zero = [jnp.zeros((1, lanes), F32)] * basis
    return lax.fori_loop(0, groups, one, (zero, zero), unroll=groups <= 8)


def modulate(readout, groups, labels, place_ref, owner_ref, bounds_ref, init_ref, far_ref, *refs):
    piece_refs, refs = refs[: len(labels)], refs[len(labels) :]
    coef_ref, *out_refs, image_ref, table_ref, parts_ref, sems = refs
    copies = [pltpu.make_async_copy(far_ref.at[t], parts_ref.at[t], sems.at[t]) for t in range(far_ref.shape[0])]
    for copy in copies:
        copy.start()
    frames, segs, _, side, _ = parts_ref.shape
    basis = init_ref.shape[0]
    owners = len(out_refs)
    rows = side // owners
    half = side // 2
    me = owner_ref[0]
    edges = edges_of(bounds_ref, readout, segs)
    times = [(edges[l] + edges[l + 1] - 1).astype(F32) / (2.0 * readout) for l in range(segs)]
    sums, own = increments(frames, basis, groups, labels, place_ref[0], piece_refs, table_ref)
    running = []
    for b in range(basis):
        total = sums[b][:, :1]
        for t in range(1, frames):
            total = total + sums[b][:, 2 * t : 2 * t + 1]
        running.append(total)
    coef = []
    for t in range(frames):
        for b in range(basis):
            running[b] = running[b] + own[b][:, 2 * t : 2 * t + 1]
            value = init_ref[b] + running[b]
            coef.append(value)
            coef_ref[pl.ds(t * basis + b, 1), :] = jnp.broadcast_to(value, (1, coef_ref.shape[1]))
    lane = lax.broadcasted_iota(jnp.int32, (1, 128), 1)
    base = jnp.zeros((1, 128), F32)
    slope = jnp.zeros((1, 128), F32)
    scale = jnp.zeros((1, 128), F32)
    for t in range(frames):
        for l in range(segs):
            here = lane == t * segs + l
            base = jnp.where(here, coef[t * basis], base)
            slope = jnp.where(here, coef[t * basis + 1], slope)
            scale = jnp.where(here, times[l], scale)
    down_pos = (lax.broadcasted_iota(jnp.int32, (side, 128), 0) - half).astype(F32) / half
    down = (base + slope * down_pos) * scale
    cos_down, sin_down = jnp.cos(down), jnp.sin(down)
    across_pos = (lax.broadcasted_iota(jnp.int32, (1, side), 1) - half).astype(F32) / half
    across = jnp.concatenate(
        [coef[t * basis + 2] * across_pos * times[l] for t in range(frames) for l in range(segs)], axis=0
    )
    cos_across, sin_across = jnp.cos(across), jnp.sin(across)
    for t in range(frames):
        copies[t].wait()
        image_re = jnp.zeros((side, side), F32)
        image_im = jnp.zeros((side, side), F32)
        for l in range(segs):
            n = t * segs + l
            cr, sr = cos_down[:, n : n + 1], sin_down[:, n : n + 1]
            cc, sc = cos_across[n : n + 1], sin_across[n : n + 1]
            cos = cr * cc - sr * sc
            sin = sr * cc + cr * sc
            re, im = parts_ref[t, l, 0], parts_ref[t, l, 1]
            image_re += cos * re - sin * im
            image_im += sin * re + cos * im
        image_ref[0] = image_re
        image_ref[1] = image_im
        for d, out_ref in enumerate(out_refs):
            owned = pl.multiple_of(lax.rem(me + d, owners) * rows, rows)
            out_ref[t] = image_ref[:, pl.ds(owned, rows), :]


def around(block, axis, distance):
    count = lax.axis_size(axis)
    return lax.ppermute(block, axis, [(i, (i + distance) % count) for i in range(count)])


def exchanged(block, axis, distance):
    return lax.ppermute(block, axis, [(i, i ^ distance) for i in range(lax.axis_size(axis))])


def exchange_rounds(axis, first, size):
    rounds = []
    while first < size:
        rounds.append((axis, (2 * first, 3 * first, first) if 2 * first < size else (first,)))
        first *= 4
    return rounds


def local(kdata, angles, kernels, seg_bounds, sensitivity, ref_center, projection, init_coef):
    frames, coils, _, spokes, readout = kdata.shape
    side = kernels.shape[3]
    segs = seg_bounds.shape[0] + 1
    basis = projection.shape[0]
    owners = lax.axis_size("coils")
    starts, width = windows(readout, segs)
    right, left = (jnp.stack(jnp.split(jnp.asarray(table), 2, axis=1)) for table in dft_tables(side))
    kd = jnp.swapaxes(kdata, 2, 3)
    smem = pl.BlockSpec(memory_space=pltpu.SMEM)
    vmem = pl.BlockSpec(memory_space=pltpu.VMEM)
    place = lax.axis_index("frames").astype(jnp.int32)
    owner = lax.axis_index("coils").astype(jnp.int32)

    lanes = 128
    padded = (coils + 7) // 8 * 8
    share = pl.pallas_call(
        centres,
        grid=(1,),
        out_shape=jax.ShapeDtypeStruct((padded, lanes), F32),
        in_specs=[
            pl.BlockSpec((frames, coils, spokes, 2, lanes), lambda i: (0, 0, 0, 0, readout // 2 // lanes)),
            smem,
            smem,
        ],
        out_specs=pl.BlockSpec((padded, lanes), lambda i: (0, 0)),
        scratch_shapes=[pltpu.VMEM((2 * frames, padded, lanes), F32)],
        name="centres",
    )(kd, ref_center.T, projection)

    groups = lax.axis_size("frames")
    rounds = [("frames", (1,))] + exchange_rounds("frames", 2, groups) + exchange_rounds("coils", 1, owners)
    pieces, labels = [share[None]], [[(0, 0)]]
    for axis, distances in rounds:
        held = jnp.concatenate(pieces, axis=0) if len(pieces) > 1 else pieces[0]
        names = [name for piece in labels for name in piece]
        pieces, labels = [held], [names]
        for distance in distances:
            pieces.append(exchanged(held, axis, distance))
            labels.append([(f ^ distance, c) if axis == "frames" else (f, c ^ distance) for f, c in names])

    parts = pl.pallas_call(
        functools.partial(grid_frames, starts, width, 0, frames),
        out_shape=jax.ShapeDtypeStruct((frames, segs, 2, side, side), F32),
        in_specs=[smem, smem] + [pl.BlockSpec(memory_space=pl.ANY)] * 5,
        out_specs=pl.BlockSpec(memory_space=pl.ANY),
        scratch_shapes=[pltpu.VMEM(a.shape, a.dtype) for a in (kd, kernels, right, left, sensitivity)]
        + [pltpu.VMEM((frames, segs, 2, side, side), F32), pltpu.SemaphoreType.DMA((5, 8)), pltpu.SemaphoreType.DMA((frames,))],
        name="gridding",
    )(angles, seg_bounds, kd, kernels, right, left, sensitivity)

    block = jax.ShapeDtypeStruct((frames, 2, side // owners, side), F32)
    height = (frames * basis + 7) // 8 * 8
    coef, *blocks = pl.pallas_call(
        functools.partial(modulate, readout, groups, labels),
        out_shape=(jax.ShapeDtypeStruct((height, lanes), F32),) + (block,) * owners,
        in_specs=[smem, smem, smem, smem, pl.BlockSpec(memory_space=pl.ANY)] + [vmem] * len(pieces),
        out_specs=(vmem,) * (1 + owners),
        scratch_shapes=[
            pltpu.VMEM((2, side, side), F32),
            pltpu.VMEM((groups, owners, padded, lanes), F32),
            pltpu.VMEM(parts.shape, F32),
            pltpu.SemaphoreType.DMA((frames,)),
        ],
        compiler_params=pltpu.CompilerParams(vmem_limit_bytes=52 * 2**20),
        name="modulate",
    )(place.reshape(1), owner.reshape(1), seg_bounds, init_coef, parts, *pieces)
    image = blocks[0]
    for d in range(1, owners):
        image = image + around(blocks[d], "coils", d)
    field_coef = coef[: frames * basis, 0].reshape(frames, basis)
    return (image, field_coef)


def solution(mesh):
    placed = (
        P("frames", "coils", None, None, None),
        P("frames", None),
        P(),
        P(),
        P("coils", None, None, None),
        P("coils", None),
        P(None, "coils"),
        P(),
    )
    def located(*arguments):
        with jax.sharding.use_abstract_mesh(mesh.abstract_mesh):
            return local(*arguments)

    return jax.shard_map(
        local,
        mesh=mesh,
        in_specs=placed,
        out_specs=(P("frames", None, "coils", None), P("frames", None)),
        check_vma=False,
    )
```
